32 devices in a mesh: vox: 16 (over z, y, x), tm: 2 (over core).
Axes of the slice: x: 2, y: 2, z: 4, core: 2. Of those that a mesh axis runs over, the one named last changes fastest.
Arguments:
- movie: bfloat16 [32768, 1024], P('vox', 'tm'), may hold values from -192 to 192
- footprints: bfloat16 [128, 32768], P(None, 'vox'), may hold values from 0 to 1
- traces: bfloat16 [128, 1024], P(None, 'tm'), may hold values from -3 to 3
- support: int32 [128, 256], P(None, 'vox'), may hold values 0 or 1
- block_order: int32 [8], replicated, may hold values from 0 to 7, each once
Outputs:
- new_footprints: bfloat16 [128, 32768], P(None, 'vox')
- new_traces: float32 [128, 1024], P(None, 'tm')
The draws below stay inside these ranges and needn't reach their ends.
Inputs may be any that keep to these rules, and one draw needn't show every extreme that they name: block_order holds each block number exactly once.
All inputs are finite; a program needn't handle non-finite values. No bound on the sum of `support` on one device may be relied on, other than what follows from the above.
Results may differ from the reference program's by a relative error of at most 0.011.
Values may be sent and summed in bfloat16 or wider, within the bound.
No kernel may reach another device: no remote copies, remote signals or barrier semaphores. Data moves between devices by JAX's collectives and lax.ppermute only.
A program may use at most 64 MiB of HBM per device.

```python
import jax
import jax.numpy as jnp
from jax import lax

K = 128
BLOCKC = 16
NBLK = 8
YR = 16
XC = 128
INNER = 3
NZ = 16
MROWS = 256
VOXELS = 32768
FRAMES = 1024


def with_ends(array, key, smallest, largest):
    index_at = [jax.random.randint(jax.random.fold_in(key, axis), (), 0, length) for axis, length in enumerate(array.shape)]
    longest = array.shape.index(max(array.shape))
    next_to = index_at[:longest] + [(index_at[longest] + 1) % array.shape[longest]] + index_at[longest + 1:]
    return array.at[tuple(index_at)].set(smallest).at[tuple(next_to)].set(largest)


def level_of(key, shape, pieces, low, high):
    def one(axis_at, parts):
        draws = jax.random.uniform(jax.random.fold_in(jax.random.fold_in(key, 6), axis_at), (parts,), jnp.float32, low / len(pieces), high / len(pieces))
        return jnp.repeat(jnp.exp(draws), shape[axis_at] // parts).reshape((-1,) + (1,) * (len(shape) - axis_at - 1))

    factor_of = one(*pieces[0])
    for cut in pieces[1:]:
        factor_of = factor_of * one(*cut)
    return factor_of


def noise(key, extent, width, bound, shards=(), kind=jnp.bfloat16):
    drawn = width * jax.random.normal(key, extent, jnp.float32)
    if shards:
        drawn = drawn * level_of(key, extent, shards, -0.22, 0.18)
    return jnp.clip(drawn, -bound, bound).astype(kind)


def setup_inputs(seed: int = 0) -> dict:
    arg_keys = jax.random.split(jax.random.key(seed), 6)
    return {
        "movie": noise(arg_keys[0], (VOXELS, FRAMES), 32.0, 192.0, ((0, 16), (1, 2))),
        "footprints": jnp.clip(1.0 * jax.random.uniform(arg_keys[1], (K, VOXELS), jnp.float32) ** level_of(arg_keys[1], (K, VOXELS), ((1, 16),), -0.2, 0.2), 0.0, 1.0).astype(jnp.bfloat16),
        "traces": noise(arg_keys[2], (K, FRAMES), 0.5, 3.0, ((1, 2),)),
        "support": with_ends((jax.random.randint(arg_keys[3], (K, MROWS), 0, 3) < 1).astype(jnp.int32), jax.random.fold_in(arg_keys[3], 1), 0, 1),
        "block_order": jax.random.permutation(arg_keys[4], NBLK).astype(jnp.int32),
    }


smooth_weight = 256.0
ridge_weight = 2048.0


def laplace_full(grid):
    padded = jnp.pad(grid, ((0, 0), (1, 1), (1, 1), (1, 1)))
    center = padded[:, 1:-1, 1:-1, 1:-1]
    beside = padded[:, 2:, 1:-1, 1:-1] + padded[:, :-2, 1:-1, 1:-1]
    beside = beside + padded[:, 1:-1, 2:, 1:-1] + padded[:, 1:-1, :-2, 1:-1]
    beside = beside + padded[:, 1:-1, 1:-1, 2:] + padded[:, 1:-1, 1:-1, :-2]
    return smooth_weight * (6.0 * center - beside)


def footprint_sweep(weights, correlation, smoothing, kept_mask, trace_gram, block_order):
    diagonal_f = jnp.diagonal(trace_gram) + 6.0 * smooth_weight

    def advance(position, current):
        start = (block_order[position] * BLOCKC).astype(jnp.int32)
        gram_rows = lax.dynamic_slice_in_dim(trace_gram, start, BLOCKC, 0)
        block_now = lax.dynamic_slice_in_dim(current, start, BLOCKC, 0)
        corr_rows = lax.dynamic_slice_in_dim(correlation, start, BLOCKC, 0)
        smooth_rows = lax.dynamic_slice_in_dim(smoothing, start, BLOCKC, 0)
        mask_rows = lax.dynamic_slice_in_dim(kept_mask, start, BLOCKC, 0)
        scale_rows = lax.dynamic_slice_in_dim(diagonal_f, start, BLOCKC, 0)
        product = jnp.dot(gram_rows, current, precision=lax.Precision.HIGHEST)
        updated = mask_rows * jnp.maximum(block_now + (corr_rows - product - smooth_rows) / scale_rows[:, None], 0.0)
        return lax.dynamic_update_slice_in_dim(current, updated, start, 0)

    for sweep_pass in range(INNER):
        weights = lax.fori_loop(0, block_order.shape[0], advance, weights)
    return weights


def trace_sweep(values, projection, cross, block_order):
    diagonal_c = jnp.diagonal(cross) + ridge_weight

    def advance(position, current):
        start = (block_order[position] * BLOCKC).astype(jnp.int32)
        cross_rows = lax.dynamic_slice_in_dim(cross, start, BLOCKC, 0)
        block_now = lax.dynamic_slice_in_dim(current, start, BLOCKC, 0)
        proj_rows = lax.dynamic_slice_in_dim(projection, start, BLOCKC, 0)
        scale_rows = lax.dynamic_slice_in_dim(diagonal_c, start, BLOCKC, 0)
        product = jnp.dot(cross_rows, current, precision=lax.Precision.HIGHEST)
        updated = jnp.maximum(block_now + (proj_rows - product - ridge_weight * block_now) / scale_rows[:, None], 0.0)
        return lax.dynamic_update_slice_in_dim(current, updated, start, 0)

    for sweep_pass in range(INNER):
        values = lax.fori_loop(0, block_order.shape[0], advance, values)
    return values


def reference(movie, footprints, traces, support, block_order):
    comps, voxels = footprints.shape
    grid = footprints.astype(jnp.float32).reshape(comps, NZ, YR, XC)
    smoothing = laplace_full(grid).reshape(comps, voxels)
    kept_mask = jnp.broadcast_to(support.astype(jnp.float32)[:, :, None], (comps, NZ * YR, XC)).reshape(comps, voxels)
    correlation = lax.dot_general(traces, movie, (((1,), (1,)), ((), ())), preferred_element_type=jnp.float32)
    trace_gram = lax.dot_general(traces, traces, (((1,), (1,)), ((), ())), preferred_element_type=jnp.float32)
    start_fp = footprints.astype(jnp.float32) * kept_mask
    new_footprints = footprint_sweep(start_fp, correlation, smoothing, kept_mask, trace_gram, block_order).astype(jnp.bfloat16)
    projection = jnp.dot(new_footprints, movie, preferred_element_type=jnp.float32)
    cross = lax.dot_general(new_footprints, new_footprints, (((1,), (1,)), ((), ())), preferred_element_type=jnp.float32)
    new_traces = trace_sweep(traces.astype(jnp.float32), projection, cross, block_order)
    return (new_footprints, new_traces)
```

```python
import functools

import jax
import jax.numpy as jnp
from jax import lax
from jax.experimental import pallas as pl
from jax.experimental.pallas import tpu as pltpu
from jax.sharding import PartitionSpec as P

BLOCKC = 16
XC = 128
INNER = 3

smooth_weight = 256.0
ridge_weight = 2048.0

F32 = jnp.float32
BF16 = jnp.bfloat16
VMEM = pl.BlockSpec(memory_space=pltpu.VMEM)
SMEM = pl.BlockSpec(memory_space=pltpu.SMEM)


def split_rows(system, gs_ref):
    comps = system.shape[0]
    high = system.astype(BF16)
    low = (system - high.astype(F32)).astype(BF16)
    for start in range(0, comps, BLOCKC):
        rows = slice(start, start + BLOCKC)
        for side in range(2):
            lanes = slice(side * comps, (side + 1) * comps)
            gs_ref[2 * start : 2 * start + BLOCKC, lanes] = high[rows]
            gs_ref[2 * start + BLOCKC : 2 * start + 2 * BLOCKC, lanes] = low[rows]


def diagonal_of(gram):
    row = lax.broadcasted_iota(jnp.int32, gram.shape, 0)
    col = lax.broadcasted_iota(jnp.int32, gram.shape, 1)
    eye = row == col
    return eye, jnp.sum(jnp.where(eye, gram, 0.0), axis=1, keepdims=True)


def sweep_steps(order_ref, gs_ref, target_ref, stacked_ref, keep_ref=None, out_ref=None):
    comps = target_ref.shape[0]
    blocks = comps // BLOCKC
    for step in range(INNER * blocks):
        block = order_ref[step % blocks]
        rows = pl.ds(pl.multiple_of(block * BLOCKC, BLOCKC), BLOCKC)
        low_rows = pl.ds(pl.multiple_of(comps + block * BLOCKC, BLOCKC), BLOCKC)
        pair = pl.ds(pl.multiple_of(block * 2 * BLOCKC, 2 * BLOCKC), 2 * BLOCKC)
        product = jnp.dot(gs_ref[pair, :], stacked_ref[...], preferred_element_type=F32)
        updated = jnp.maximum(target_ref[rows, :] + (product[:BLOCKC] + product[BLOCKC:]), 0.0)
        if keep_ref is not None:
            updated = updated * keep_ref[rows, :]
        high = updated.astype(BF16)
        stacked_ref[rows, :] = high
        stacked_ref[low_rows, :] = (updated - high.astype(F32)).astype(BF16)
        if out_ref is not None:
            out_ref[rows, :] = updated


def prepare_kernel(corr_ref, gram_ref, fp_ref, support_ref, target_ref, keep_ref, gs_ref, scale_ref):
    comps, share = corr_ref.shape
    me = lax.axis_index("tm")
    count = fp_ref.shape[1] // share
    first = me * share
    gram = gram_ref[...]
    eye, diagonal = diagonal_of(gram)
    inverse = 1.0 / (diagonal + 6.0 * smooth_weight)
    split_rows(jnp.where(eye, 6.0 * smooth_weight * inverse, -gram * inverse), gs_ref)
    scale_ref[...] = jnp.broadcast_to(smooth_weight * inverse, scale_ref.shape)

    lane = lax.broadcasted_iota(jnp.int32, (comps, XC), 1)
    column = lax.broadcasted_iota(jnp.int32, support_ref.shape, 1)
    support = support_ref[...].astype(F32)

    def row_at(offset):
        at = pl.multiple_of(first + offset, XC)
        return fp_ref[:, pl.ds(at, XC)].astype(F32)

    below = pl.multiple_of(jnp.maximum(first - XC, 0), XC)
    above = pl.multiple_of(jnp.minimum(first + share, fp_ref.shape[1] - XC), XC)
    before = fp_ref[:, pl.ds(below, XC)].astype(F32) * jnp.where(me > 0, 1.0, 0.0)
    center = row_at(0)
    for offset in range(0, share, XC):
        if offset + XC < share:
            after = row_at(offset + XC)
        else:
            after = fp_ref[:, pl.ds(above, XC)].astype(F32) * jnp.where(me < count - 1, 1.0, 0.0)
        left = jnp.where(lane == 0, 0.0, pltpu.roll(center, 1, 1))
        right = jnp.where(lane == XC - 1, 0.0, pltpu.roll(center, XC - 1, 1))
        beside = before + after + left + right
        smoothing = smooth_weight * (6.0 * center - beside)
        lanes = slice(offset, offset + XC)
        target_ref[:, lanes] = (corr_ref[:, lanes] - smoothing) * inverse
        here = me * (share // XC) + offset // XC
        kept = jnp.sum(jnp.where(column == here, support, 0.0), axis=1, keepdims=True)
        keep_ref[:, lanes] = jnp.broadcast_to(kept, (comps, XC))
        before, center = center, after


def footprint_kernel(order_ref, target_ref, keep_ref, gs_ref, scale_ref, fp_ref, head_ref, tail_ref, out_ref, goal_ref, stacked_ref):
    comps, share = target_ref.shape
    me = lax.axis_index("tm")
    for offset in range(0, share, XC):
        lanes = slice(offset, offset + XC)
        sides = head_ref[:, lanes].astype(F32) + tail_ref[:, lanes].astype(F32)
        goal_ref[:, lanes] = target_ref[:, lanes] + sides * scale_ref[...]
        at = pl.multiple_of(me * share + offset, XC)
        center = fp_ref[:, pl.ds(at, XC)].astype(F32)
        stacked_ref[:comps, lanes] = (center * keep_ref[:, lanes]).astype(BF16)
    stacked_ref[comps:, :] = jnp.zeros((comps, share), BF16)
    sweep_steps(order_ref, gs_ref, goal_ref, stacked_ref, keep_ref)
    out_ref[...] = stacked_ref[:comps, :]


def product_kernel(pieces, frames, *refs):
    piece_refs, movie_ref, joined_ref, full_ref = refs[:pieces], refs[pieces], refs[pieces + 1], refs[pieces + 2]
    me = lax.axis_index("tm")
    projection = cross = None
    for index, ref in enumerate(piece_refs):
        width = ref.shape[1]
        place = pl.multiple_of((me if index == 0 else 1 - me) * width, width) if pieces > 1 else 0
        piece = ref[...]
        full_ref[:, pl.ds(place, width)] = piece
        part = jnp.dot(piece, movie_ref[pl.ds(place, width), :], preferred_element_type=F32)
        own = lax.dot_general(piece, piece, (((1,), (1,)), ((), ())), preferred_element_type=F32)
        projection = part if projection is None else projection + part
        cross = own if cross is None else cross + own
    joined_ref[:, :frames] = projection
    joined_ref[:, frames:] = cross


def trace_kernel(order_ref, joined_ref, traces_ref, out_ref, goal_ref, gs_ref, stacked_ref):
    comps, frames = traces_ref.shape
    cross = joined_ref[:, frames:]
    eye, diagonal = diagonal_of(cross)
    inverse = 1.0 / (diagonal + ridge_weight)
    split_rows(jnp.where(eye, 0.0, -cross * inverse), gs_ref)
    goal_ref[...] = joined_ref[:, :frames] * inverse
    stacked_ref[:comps, :] = traces_ref[...]
    stacked_ref[comps:, :] = jnp.zeros((comps, frames), BF16)
    sweep_steps(order_ref, gs_ref, goal_ref, stacked_ref, None, out_ref)


def shape_of(dims, dtype):
    return jax.ShapeDtypeStruct(dims, dtype)


def swap(array):
    return lax.ppermute(array, "tm", [(0, 1), (1, 0)])


def sum_over_vox(joined):
    count = lax.axis_size("vox")
    comps, width = joined.shape
    if comps % count:
        return lax.psum(joined, "vox")
    parts = lax.all_to_all(joined, "vox", 0, 0, tiled=True)
    mine = jnp.sum(parts.reshape(count, comps // count, width), axis=0)
    spread = jnp.broadcast_to(mine[None], (count, comps // count, width)).reshape(comps, width)
    return lax.all_to_all(spread, "vox", 0, 0, tiled=True)


def local(movie, footprints, traces, support, block_order):
    comps, vox_local = footprints.shape
    frames = traces.shape[1]
    cores = lax.axis_size("tm")
    planes = lax.axis_size("vox")
    share = vox_local // cores
    me = lax.axis_index("tm")

    own = lax.dynamic_slice_in_dim(footprints, me * share, share, 1)
    head = lax.ppermute(own, "vox", [(i, i + 1) for i in range(planes - 1)])
    tail = lax.ppermute(own, "vox", [(i + 1, i) for i in range(planes - 1)])

    correlation = lax.dot_general(traces, movie, (((1,), (1,)), ((), ())), preferred_element_type=F32)
    gram = lax.dot_general(traces, traces, (((1,), (1,)), ((), ())), preferred_element_type=F32)
    if cores == 2:
        theirs = lax.dynamic_slice_in_dim(correlation, (1 - me) * share, share, 1)
        ours = lax.dynamic_slice_in_dim(correlation, me * share, share, 1)
        correlation = ours + swap(theirs)
        gram = gram + swap(gram)
    else:
        correlation = lax.psum_scatter(correlation, "tm", scatter_dimension=1, tiled=True)
        gram = lax.psum(gram, "tm")

    target, keep, system, scale = pl.pallas_call(
        prepare_kernel,
        out_shape=[
            shape_of((comps, share), F32),
            shape_of((comps, share), F32),
            shape_of((2 * comps, 2 * comps), BF16),
            shape_of((comps, XC), F32),
        ],
        in_specs=[VMEM] * 4,
        out_specs=[VMEM] * 4,
        cost_estimate=pl.CostEstimate(flops=20 * comps * share, bytes_accessed=16 * comps * share, transcendentals=0),
    )(correlation, gram, footprints, support)

    half = pl.pallas_call(
        footprint_kernel,
        out_shape=shape_of((comps, share), BF16),
        in_specs=[SMEM] + [VMEM] * 7,
        out_specs=VMEM,
        scratch_shapes=[pltpu.VMEM((comps, share), F32), pltpu.VMEM((2 * comps, share), BF16)],
    )(block_order, target, keep, system, scale, footprints, head, tail)

    if cores == 2:
        pieces = [half, swap(half)]
    else:
        pieces = [lax.all_gather(half, "tm", axis=1, tiled=True)]
    joined, new_footprints = pl.pallas_call(
        functools.partial(product_kernel, len(pieces), frames),
        out_shape=[shape_of((comps, frames + comps), F32), shape_of((comps, vox_local), BF16)],
        in_specs=[VMEM] * (len(pieces) + 1),
        out_specs=[VMEM] * 2,
    )(*pieces, movie)

    joined = sum_over_vox(joined)
    new_traces = pl.pallas_call(
        trace_kernel,
        out_shape=shape_of((comps, frames), F32),
        in_specs=[SMEM] + [VMEM] * 2,
        out_specs=VMEM,
        scratch_shapes=[
            pltpu.VMEM((comps, frames), F32),
            pltpu.VMEM((2 * comps, 2 * comps), BF16),
            pltpu.VMEM((2 * comps, frames), BF16),
        ],
    )(block_order, joined, traces)
    return (new_footprints, new_traces)


def solution(mesh):
    placed = (P("vox", "tm"), P(None, "vox"), P(None, "tm"), P(None, "vox"), P())
    return jax.shard_map(
        local,
        mesh=mesh,
        in_specs=placed,
        out_specs=(P(None, "vox"), P(None, "tm")),
        check_vma=False,
    )
```

```python
import functools

import jax
import jax.numpy as jnp
from jax import lax
from jax.experimental import pallas as pl
from jax.experimental.pallas import tpu as pltpu
from jax.sharding import PartitionSpec as P

BLOCKC = 16
XC = 128
INNER = 3
GROUP = 4

smooth_weight = 256.0
ridge_weight = 2048.0

F32 = jnp.float32
BF16 = jnp.bfloat16
VMEM = pl.BlockSpec(memory_space=pltpu.VMEM)
SMEM = pl.BlockSpec(memory_space=pltpu.SMEM)
ANY = pl.BlockSpec(memory_space=pl.ANY)
SMALL = pltpu.CompilerParams(vmem_limit_bytes=12 * 1024 * 1024)
BY_LAST = (((1,), (1,)), ((), ()))


def shape_of(dims, dtype):
    return jax.ShapeDtypeStruct(dims, dtype)


def split_rows(system, gs_ref):
    comps = system.shape[0]
    high = system.astype(BF16)
    low = (system - high.astype(F32)).astype(BF16)
    for start in range(0, comps, BLOCKC):
        rows = slice(start, start + BLOCKC)
        for side in range(2):
            lanes = slice(side * comps, (side + 1) * comps)
            gs_ref[2 * start : 2 * start + BLOCKC, lanes] = high[rows]
            gs_ref[2 * start + BLOCKC : 2 * start + 2 * BLOCKC, lanes] = low[rows]


def diagonal_of(gram):
    row = lax.broadcasted_iota(jnp.int32, gram.shape, 0)
    col = lax.broadcasted_iota(jnp.int32, gram.shape, 1)
    eye = row == col
    return eye, jnp.sum(jnp.where(eye, gram, 0.0), axis=1, keepdims=True)


def sweep_steps(order_ref, gs_ref, target_ref, stacked_ref, keep_ref=None, out_ref=None):
    comps = target_ref.shape[0]
    blocks = comps // BLOCKC
    for step in range(INNER * blocks):
        block = order_ref[step % blocks]
        rows = pl.ds(pl.multiple_of(block * BLOCKC, BLOCKC), BLOCKC)
        low_rows = pl.ds(pl.multiple_of(comps + block * BLOCKC, BLOCKC), BLOCKC)
        pair = pl.ds(pl.multiple_of(block * 2 * BLOCKC, 2 * BLOCKC), 2 * BLOCKC)
        product = jnp.dot(gs_ref[pair, :], stacked_ref[...], preferred_element_type=F32)
        updated = jnp.maximum(target_ref[rows, :] + (product[:BLOCKC] + product[BLOCKC:]), 0.0)
        if keep_ref is not None:
            updated = updated * keep_ref[rows, :]
        high = updated.astype(BF16)
        stacked_ref[rows, :] = high
        stacked_ref[low_rows, :] = (updated - high.astype(F32)).astype(BF16)
        if out_ref is not None:
            out_ref[rows, :] = updated


def movie_copies(movie_refs, movie_bufs, sems):
    copies = []
    for index, (ref, buf) in enumerate(zip(movie_refs, movie_bufs)):
        share = buf.shape[0]
        place = lax.axis_index("tm") * share if ref.shape[0] > share else 0
        copies.append(pltpu.make_async_copy(ref.at[pl.ds(place, share), :], buf, sems.at[index]))
    return copies


def prepare_kernel(pieces, *refs):
    trace_refs, movie_refs, refs = refs[:pieces], refs[pieces : 2 * pieces], refs[2 * pieces :]
    fp_ref, support_ref, target_ref, keep_ref, gs_ref, scale_ref = refs[:6]
    movie_bufs, sems = refs[6:-1], refs[-1]
    comps, share = target_ref.shape
    copies = movie_copies(movie_refs, movie_bufs, sems)
    for copy in copies:
        copy.start()

    me = lax.axis_index("tm")
    count = fp_ref.shape[1] // share
    first = me * share
    gram = None
    for ref in trace_refs:
        part = lax.dot_general(ref[...], ref[...], BY_LAST, preferred_element_type=F32)
        gram = part if gram is None else gram + part
    eye, diagonal = diagonal_of(gram)
    inverse = 1.0 / (diagonal + 6.0 * smooth_weight)
    split_rows(jnp.where(eye, 6.0 * smooth_weight * inverse, -gram * inverse), gs_ref)
    scale_ref[...] = jnp.broadcast_to(smooth_weight * inverse, scale_ref.shape)

    lane = lax.broadcasted_iota(jnp.int32, (comps, XC), 1)
    column = lax.broadcasted_iota(jnp.int32, support_ref.shape, 1)
    support = support_ref[...].astype(F32)

    def row_at(offset):
        at = pl.multiple_of(first + offset, XC)
        return fp_ref[:, pl.ds(at, XC)].astype(F32)

    below = pl.multiple_of(jnp.maximum(first - XC, 0), XC)
    above = pl.multiple_of(jnp.minimum(first + share, fp_ref.shape[1] - XC), XC)
    before = fp_ref[:, pl.ds(below, XC)].astype(F32) * jnp.where(me > 0, 1.0, 0.0)
    center = row_at(0)
    for offset in range(0, share, XC):
        if offset + XC < share:
            after = row_at(offset + XC)
        else:
            after = fp_ref[:, pl.ds(above, XC)].astype(F32) * jnp.where(me < count - 1, 1.0, 0.0)
        left = jnp.where(lane == 0, 0.0, pltpu.roll(center, 1, 1))
        right = jnp.where(lane == XC - 1, 0.0, pltpu.roll(center, XC - 1, 1))
        beside = before + after + left + right
        lanes = slice(offset, offset + XC)
        target_ref[:, lanes] = smooth_weight * (6.0 * center - beside)
        here = me * (share // XC) + offset // XC
        kept = jnp.sum(jnp.where(column == here, support, 0.0), axis=1, keepdims=True)
        keep_ref[:, lanes] = jnp.broadcast_to(kept, (comps, XC))
        before, center = center, after

    for copy in copies:
        copy.wait()
    correlation = None
    for ref, buf in zip(trace_refs, movie_bufs):
        part = lax.dot_general(ref[...], buf[...], BY_LAST, preferred_element_type=F32)
        correlation = part if correlation is None else correlation + part
    target_ref[...] = (correlation - target_ref[...]) * inverse


def footprint_kernel(pieces, order_ref, target_ref, keep_ref, gs_ref, scale_ref, fp_ref, head_ref, tail_ref, *refs):
    movie_refs, half_ref, joined_refs, refs = refs[:pieces], refs[pieces], refs[pieces + 1 : 2 * pieces + 1], refs[2 * pieces + 1 :]
    goal_ref, stacked_ref, movie_bufs, sems = refs[0], refs[1], refs[2:-1], refs[-1]
    comps, share = target_ref.shape
    copies = movie_copies(movie_refs, movie_bufs, sems)
    for copy in copies:
        copy.start()
    me = lax.axis_index("tm")
    for offset in range(0, share, XC):
        lanes = slice(offset, offset + XC)
        sides = head_ref[:, lanes].astype(F32) + tail_ref[:, lanes].astype(F32)
        goal_ref[:, lanes] = target_ref[:, lanes] + sides * scale_ref[...]
        at = pl.multiple_of(me * share + offset, XC)
        center = fp_ref[:, pl.ds(at, XC)].astype(F32)
        stacked_ref[:comps, lanes] = (center * keep_ref[:, lanes]).astype(BF16)
    stacked_ref[comps:, :] = jnp.zeros((comps, share), BF16)
    sweep_steps(order_ref, gs_ref, goal_ref, stacked_ref, keep_ref)
    half = stacked_ref[:comps, :]
    half_ref[...] = half
    for copy in copies:
        copy.wait()
    cross = lax.dot_general(half, half, BY_LAST, preferred_element_type=F32)
    for buf, joined_ref in zip(movie_bufs, joined_refs):
        frames = buf.shape[1]
        joined_ref[:, :frames] = jnp.dot(half, buf[...], preferred_element_type=F32)
        joined_ref[:, frames:] = cross


def chunk_kernel(stride, ours_ref, theirs_ref, *out_refs):
    rows = out_refs[0].shape[0]
    digit = lax.axis_index("vox") // stride % GROUP
    for index, out_ref in enumerate(out_refs):
        at = pl.ds(pl.multiple_of((digit ^ index) * rows, rows), rows)
        out_ref[...] = ours_ref[at, :] + theirs_ref[at, :]


def trace_kernel(order_ref, traces_ref, *refs):
    joined_refs, (out_ref, joined, goal_ref, gs_ref, stacked_ref) = refs[:-5], refs[-5:]
    comps, frames = traces_ref.shape
    digit = lax.axis_index("vox") % GROUP
    for index, ref in enumerate(joined_refs):
        rows = ref.shape[0]
        place = pl.multiple_of((digit ^ index) * rows, rows) if rows < comps else 0
        joined[pl.ds(place, rows), :] = ref[...]
    cross = joined[:, frames:]
    eye, diagonal = diagonal_of(cross)
    inverse = 1.0 / (diagonal + ridge_weight)
    split_rows(jnp.where(eye, 0.0, -cross * inverse), gs_ref)
    goal_ref[...] = joined[:, :frames] * inverse
    stacked_ref[:comps, :] = traces_ref[...]
    stacked_ref[comps:, :] = jnp.zeros((comps, frames), BF16)
    sweep_steps(order_ref, gs_ref, goal_ref, stacked_ref, None, out_ref)


def swap(array):
    return lax.ppermute(array, "tm", [(0, 1), (1, 0)])


def from_group(arrays, stride):
    count = lax.axis_size("vox")
    return [lax.ppermute(array, "vox", [(i, i ^ (k * stride)) for i in range(count)]) for k, array in arrays]


def tree_sum(own, others):
    return (own + others[0]) + (others[1] + others[2])


def sum_over_vox(ours, theirs):
    comps, width = ours.shape
    rows = comps // GROUP
    top = lax.axis_size("vox") // GROUP
    chunks = pl.pallas_call(
        functools.partial(chunk_kernel, 1),
        out_shape=[shape_of((rows, width), F32)] * GROUP,
        in_specs=[VMEM] * 2,
        compiler_params=SMALL,
        out_specs=[VMEM] * GROUP,
    )(ours, theirs)
    mine = tree_sum(chunks[0], from_group([(k, chunks[k]) for k in range(1, GROUP)], 1))
    mine = tree_sum(mine, from_group([(k, mine) for k in range(1, GROUP)], top))
    return [mine] + from_group([(k, mine) for k in range(1, GROUP)], 1)


def local(movie, footprints, traces, support, block_order):
    comps, vox_local = footprints.shape
    frames = traces.shape[1]
    cores = lax.axis_size("tm")
    planes = lax.axis_size("vox")
    share = vox_local // cores
    me = lax.axis_index("tm")

    own = lax.dynamic_slice_in_dim(footprints, me * share, share, 1)
    head = lax.ppermute(own, "vox", [(i, i + 1) for i in range(planes - 1)])
    tail = lax.ppermute(own, "vox", [(i + 1, i) for i in range(planes - 1)])
    if cores == 2:
        movies = [movie, swap(movie)]
        all_traces = [traces, swap(traces)]
    else:
        movies = [lax.all_to_all(movie, "tm", 0, 1, tiled=True)]
        all_traces = [lax.all_gather(traces, "tm", axis=1, tiled=True)]
    pieces = len(movies)
    movie_scratch = [pltpu.VMEM((share, part.shape[1]), BF16) for part in movies] + [pltpu.SemaphoreType.DMA((pieces,))]

    target, keep, system, scale = pl.pallas_call(
        functools.partial(prepare_kernel, pieces),
        out_shape=[
            shape_of((comps, share), F32),
            shape_of((comps, share), F32),
            shape_of((2 * comps, 2 * comps), BF16),
            shape_of((comps, XC), F32),
        ],
        in_specs=[VMEM] * pieces + [ANY] * pieces + [VMEM] * 2,
        compiler_params=SMALL,
        out_specs=[VMEM] * 4,
        scratch_shapes=movie_scratch,
    )(*all_traces, *movies, footprints, support)

    half, *joined = pl.pallas_call(
        functools.partial(footprint_kernel, pieces),
        out_shape=[shape_of((comps, share), BF16)]
        + [shape_of((comps, part.shape[1] + comps), F32) for part in movies],
        in_specs=[SMEM] + [VMEM] * 7 + [ANY] * pieces,
        compiler_params=SMALL,
        out_specs=[VMEM] * (pieces + 1),
        scratch_shapes=[pltpu.VMEM((comps, share), F32), pltpu.VMEM((2 * comps, share), BF16)] + movie_scratch,
    )(block_order, target, keep, system, scale, footprints, head, tail, *movies)

    if cores == 2:
        ours, theirs = joined[0], swap(joined[1])
        other = swap(half)
        new_footprints = jnp.where(
            me == 0, jnp.concatenate([half, other], axis=1), jnp.concatenate([other, half], axis=1)
        )
    else:
        joined = joined[0]
        projection = lax.psum_scatter(joined[:, : frames * cores], "tm", scatter_dimension=1, tiled=True)
        ours = jnp.concatenate([projection, lax.psum(joined[:, frames * cores :], "tm")], axis=1)
        theirs = jnp.zeros_like(ours)
        new_footprints = lax.all_gather(half, "tm", axis=1, tiled=True)

    if planes == GROUP * GROUP:
        joined = sum_over_vox(ours, theirs)
    else:
        joined = [lax.psum(ours + theirs, "vox")]
    new_traces = pl.pallas_call(
        trace_kernel,
        out_shape=shape_of((comps, frames), F32),
        in_specs=[SMEM] + [VMEM] * (len(joined) + 1),
        compiler_params=SMALL,
        out_specs=VMEM,
        scratch_shapes=[
            pltpu.VMEM((comps, frames + comps), F32),
            pltpu.VMEM((comps, frames), F32),
            pltpu.VMEM((2 * comps, 2 * comps), BF16),
            pltpu.VMEM((2 * comps, frames), BF16),
        ],
    )(block_order, traces, *joined)
    return (new_footprints, new_traces)


def solution(mesh):
    placed = (P("vox", "tm"), P(None, "vox"), P(None, "tm"), P(None, "vox"), P())
    return jax.shard_map(
        local,
        mesh=mesh,
        in_specs=placed,
        out_specs=(P(None, "vox"), P(None, "tm")),
        check_vma=False,
    )
```

```python
import functools

import jax
import jax.numpy as jnp
from jax import lax
from jax.experimental import pallas as pl
from jax.experimental.pallas import tpu as pltpu
from jax.sharding import PartitionSpec as P

BLOCKC = 16
XC = 128
INNER = 3
GROUP = 4

smooth_weight = 256.0
ridge_weight = 2048.0

F32 = jnp.float32
BF16 = jnp.bfloat16
VMEM = pl.BlockSpec(memory_space=pltpu.VMEM)
SMEM = pl.BlockSpec(memory_space=pltpu.SMEM)
ANY = pl.BlockSpec(memory_space=pl.ANY)
SMALL = pltpu.CompilerParams(vmem_limit_bytes=12 * 1024 * 1024)
BY_LAST = (((1,), (1,)), ((), ()))


def shape_of(dims, dtype):
    return jax.ShapeDtypeStruct(dims, dtype)


def split_terms(array):
    high = array.astype(BF16)
    return high, (array - high.astype(F32)).astype(BF16)


def rows_of(place):
    return slice(place * BLOCKC, (place + 1) * BLOCKC)


def rows_from(order_ref, place):
    return pl.ds(pl.multiple_of(order_ref[place] * BLOCKC, BLOCKC), BLOCKC)


def diagonal_of(gram):
    row = lax.broadcasted_iota(jnp.int32, gram.shape, 0)
    col = lax.broadcasted_iota(jnp.int32, gram.shape, 1)
    eye = row == col
    return eye, jnp.sum(jnp.where(eye, gram, 0.0), axis=1, keepdims=True)


def store_system(system, gs_ref, coef_ref):
    comps = system.shape[0]
    blocks = comps // BLOCKC
    high, low = split_terms(system)
    for place in range(blocks):
        rows = rows_of(place)
        before = (place - 1) % blocks * BLOCKC
        for side in range(2):
            lanes = slice(side * comps, (side + 1) * comps)
            gs_ref[rows_of(2 * place), lanes] = high[rows]
            gs_ref[rows_of(2 * place + 1), lanes] = low[rows]
        for k in range(BLOCKC):
            coef_ref[place, k] = jnp.broadcast_to(system[rows, before + k : before + k + 1], (BLOCKC, XC))


def sweep_steps(gs_ref, coef_ref, goal_ref, stacked_ref, value_ref, keep_ref=None):
    comps, width = goal_ref.shape
    blocks = comps // BLOCKC

    def product_of(place):
        pair = slice(2 * BLOCKC * place, 2 * BLOCKC * (place + 1))
        product = jnp.dot(gs_ref[pair, :], stacked_ref[...], preferred_element_type=F32)
        return product[:BLOCKC] + product[BLOCKC:]

    steps = INNER * blocks
    ready, change = product_of(0), None
    for step in range(steps):
        place = step % blocks
        rows = rows_of(place)
        following = product_of((step + 1) % blocks) if step + 1 < steps else None
        base = goal_ref[rows, :] + ready
        columns = []
        for lane in range(0, width, XC):
            lanes = slice(lane, lane + XC)
            total = base[:, lanes]
            if change is not None:
                parts = [None] * 4
                for k in range(BLOCKC):
                    term = coef_ref[place, k] * jnp.broadcast_to(change[k : k + 1, lanes], (BLOCKC, XC))
                    parts[k % 4] = term if parts[k % 4] is None else parts[k % 4] + term
                total = total + ((parts[0] + parts[1]) + (parts[2] + parts[3]))
            columns.append(jnp.maximum(total, 0.0))
        updated = jnp.concatenate(columns, axis=1)
        if keep_ref is not None:
            updated = updated * keep_ref[rows, :]
        change = updated - value_ref[rows, :]
        value_ref[rows, :] = updated
        high, low = split_terms(updated)
        stacked_ref[rows, :] = high
        stacked_ref[comps + place * BLOCKC : comps + (place + 1) * BLOCKC, :] = low
        ready = following


def movie_copies(movie_refs, movie_bufs, sems):
    copies = []
    for index, (ref, buf) in enumerate(zip(movie_refs, movie_bufs)):
        share = buf.shape[0]
        place = lax.axis_index("tm") * share if ref.shape[0] > share else 0
        copies.append(pltpu.make_async_copy(ref.at[pl.ds(place, share), :], buf, sems.at[index]))
    return copies


def prepare_kernel(pieces, order_ref, *refs):
    trace_refs, movie_refs, refs = refs[:pieces], refs[pieces : 2 * pieces], refs[2 * pieces :]
    fp_ref, support_ref, target_ref, keep_ref, start_ref, gs_ref, coef_ref, scale_ref = refs[:8]
    sorted_fp, sorted_support, refs = refs[8], refs[9], refs[10:]
    sorted_traces, movie_bufs, sems = refs[:pieces], refs[pieces : 2 * pieces], refs[2 * pieces]
    comps, share = target_ref.shape
    copies = movie_copies(movie_refs, movie_bufs, sems)
    for copy in copies:
        copy.start()

    for place in range(comps // BLOCKC):
        rows, source = rows_of(place), rows_from(order_ref, place)
        sorted_fp[rows, :] = fp_ref[source, :]
        sorted_support[rows, :] = support_ref[source, :].astype(F32)
        for ref, sorted_ref in zip(trace_refs, sorted_traces):
            sorted_ref[rows, :] = ref[source, :]

    me = lax.axis_index("tm")
    count = fp_ref.shape[1] // share
    first = me * share
    gram = None
    for ref in sorted_traces:
        part = lax.dot_general(ref[...], ref[...], BY_LAST, preferred_element_type=F32)
        gram = part if gram is None else gram + part
    eye, diagonal = diagonal_of(gram)
    inverse = 1.0 / (diagonal + 6.0 * smooth_weight)
    store_system(jnp.where(eye, 6.0 * smooth_weight * inverse, -gram * inverse), gs_ref, coef_ref)
    scale_ref[...] = jnp.broadcast_to(smooth_weight * inverse, scale_ref.shape)

    lane = lax.broadcasted_iota(jnp.int32, (comps, XC), 1)
    column = lax.broadcasted_iota(jnp.int32, support_ref.shape, 1)
    support = sorted_support[...]

    def row_at(offset):
        at = pl.multiple_of(first + offset, XC)
        return sorted_fp[:, pl.ds(at, XC)].astype(F32)

    below = pl.multiple_of(jnp.maximum(first - XC, 0), XC)
    above = pl.multiple_of(jnp.minimum(first + share, fp_ref.shape[1] - XC), XC)
    before = sorted_fp[:, pl.ds(below, XC)].astype(F32) * jnp.where(me > 0, 1.0, 0.0)
    center = row_at(0)
    for offset in range(0, share, XC):
        if offset + XC < share:
            after = row_at(offset + XC)
        else:
            after = sorted_fp[:, pl.ds(above, XC)].astype(F32) * jnp.where(me < count - 1, 1.0, 0.0)
        left = jnp.where(lane == 0, 0.0, pltpu.roll(center, 1, 1))
        right = jnp.where(lane == XC - 1, 0.0, pltpu.roll(center, XC - 1, 1))
        beside = before + after + left + right
        lanes = slice(offset, offset + XC)
        target_ref[:, lanes] = smooth_weight * (6.0 * center - beside)
        here = me * (share // XC) + offset // XC
        kept = jnp.sum(jnp.where(column == here, support, 0.0), axis=1, keepdims=True)
        kept = jnp.broadcast_to(kept, (comps, XC))
        keep_ref[:, lanes] = kept
        start_ref[:, lanes] = center * kept
        before, center = center, after

    for copy in copies:
        copy.wait()
    correlation = None
    for ref, buf in zip(sorted_traces, movie_bufs):
        part = lax.dot_general(ref[...], buf[...], BY_LAST, preferred_element_type=F32)
        correlation = part if correlation is None else correlation + part
    target_ref[...] = (correlation - target_ref[...]) * inverse


def footprint_kernel(pieces, order_ref, target_ref, keep_ref, start_ref, gs_ref, coef_ref, scale_ref, head_ref, tail_ref, *refs):
    movie_refs, half_ref, joined_refs, refs = refs[:pieces], refs[pieces], refs[pieces + 1 : 2 * pieces + 1], refs[2 * pieces + 1 :]
    goal_ref, value_ref, stacked_ref, movie_bufs, sems = refs[0], refs[1], refs[2], refs[3:-1], refs[-1]
    comps, share = target_ref.shape
    copies = movie_copies(movie_refs, movie_bufs, sems)
    for copy in copies:
        copy.start()
    value_ref[...] = start_ref[...]
    stacked_ref[:comps, :] = start_ref[...].astype(BF16)
    stacked_ref[comps:, :] = jnp.zeros((comps, share), BF16)
    for place in range(comps // BLOCKC):
        rows, source = rows_of(place), rows_from(order_ref, place)
        for offset in range(0, share, XC):
            lanes = slice(offset, offset + XC)
            sides = head_ref[source, lanes].astype(F32) + tail_ref[source, lanes].astype(F32)
            goal_ref[rows, lanes] = target_ref[rows, lanes] + sides * scale_ref[rows, :]
    sweep_steps(gs_ref, coef_ref, goal_ref, stacked_ref, value_ref, keep_ref)
    half = stacked_ref[:comps, :]
    for place in range(comps // BLOCKC):
        half_ref[rows_from(order_ref, place), :] = stacked_ref[rows_of(place), :]
    for copy in copies:
        copy.wait()
    cross = lax.dot_general(half, half, BY_LAST, preferred_element_type=F32)
    for buf, joined_ref in zip(movie_bufs, joined_refs):
        frames = buf.shape[1]
        joined_ref[:, :frames] = jnp.dot(half, buf[...], preferred_element_type=F32)
        joined_ref[:, frames:] = cross


def chunk_kernel(stride, ours_ref, theirs_ref, *out_refs):
    rows = out_refs[0].shape[0]
    digit = lax.axis_index("vox") // stride % GROUP
    for index, out_ref in enumerate(out_refs):
        at = pl.ds(pl.multiple_of((digit ^ index) * rows, rows), rows)
        out_ref[...] = ours_ref[at, :] + theirs_ref[at, :]


def trace_kernel(order_ref, traces_ref, *refs):
    joined_refs, (out_ref, joined, goal_ref, gs_ref, coef_ref, stacked_ref, value_ref) = refs[:-7], refs[-7:]
    comps, frames = traces_ref.shape
    digit = lax.axis_index("vox") % GROUP
    for index, ref in enumerate(joined_refs):
        rows = ref.shape[0]
        place = pl.multiple_of((digit ^ index) * rows, rows) if rows < comps else 0
        joined[pl.ds(place, rows), :] = ref[...]
    cross = joined[:, frames:]
    eye, diagonal = diagonal_of(cross)
    inverse = 1.0 / (diagonal + ridge_weight)
    store_system(jnp.where(eye, 0.0, -cross * inverse), gs_ref, coef_ref)
    goal_ref[...] = joined[:, :frames] * inverse
    for place in range(comps // BLOCKC):
        begin = traces_ref[rows_from(order_ref, place), :]
        stacked_ref[rows_of(place), :] = begin
        value_ref[rows_of(place), :] = begin.astype(F32)
    stacked_ref[comps:, :] = jnp.zeros((comps, frames), BF16)
    sweep_steps(gs_ref, coef_ref, goal_ref, stacked_ref, value_ref)
    for place in range(comps // BLOCKC):
        out_ref[rows_from(order_ref, place), :] = value_ref[rows_of(place), :]


def swap(array):
    return lax.ppermute(array, "tm", [(0, 1), (1, 0)])


def from_group(arrays, stride):
    count = lax.axis_size("vox")
    return [lax.ppermute(array, "vox", [(i, i ^ (k * stride)) for i in range(count)]) for k, array in arrays]


def tree_sum(own, others):
    return (own + others[0]) + (others[1] + others[2])


def sum_over_vox(ours, theirs):
    comps, width = ours.shape
    rows = comps // GROUP
    top = lax.axis_size("vox") // GROUP
    chunks = pl.pallas_call(
        functools.partial(chunk_kernel, 1),
        out_shape=[shape_of((rows, width), F32)] * GROUP,
        in_specs=[VMEM] * 2,
        compiler_params=SMALL,
        out_specs=[VMEM] * GROUP,
    )(ours, theirs)
    mine = tree_sum(chunks[0], from_group([(k, chunks[k]) for k in range(1, GROUP)], 1))
    mine = tree_sum(mine, from_group([(k, mine) for k in range(1, GROUP)], top))
    return [mine] + from_group([(k, mine) for k in range(1, GROUP)], 1)


def local(movie, footprints, traces, support, block_order):
    comps, vox_local = footprints.shape
    frames = traces.shape[1]
    cores = lax.axis_size("tm")
    planes = lax.axis_size("vox")
    share = vox_local // cores
    me = lax.axis_index("tm")

    own = lax.dynamic_slice_in_dim(footprints, me * share, share, 1)
    up = [(i, i + 1) for i in range(planes - 1)]
    sides = [lax.ppermute(own, "vox", up), lax.ppermute(own, "vox", [(j, i) for i, j in up])]
    if cores == 2:
        movies = [movie, swap(movie)]
        all_traces = [traces, swap(traces)]
    else:
        movies = [lax.all_to_all(movie, "tm", 0, 1, tiled=True)]
        all_traces = [lax.all_gather(traces, "tm", axis=1, tiled=True)]
    pieces = len(movies)
    movie_scratch = [pltpu.VMEM((share, part.shape[1]), BF16) for part in movies] + [pltpu.SemaphoreType.DMA((pieces,))]

    blocks = comps // BLOCKC
    table = (blocks, BLOCKC, BLOCKC, XC)
    target, keep, start, system, coef, scale = pl.pallas_call(
        functools.partial(prepare_kernel, pieces),
        out_shape=[
            shape_of((comps, share), F32),
            shape_of((comps, share), F32),
            shape_of((comps, share), F32),
            shape_of((2 * comps, 2 * comps), BF16),
            shape_of(table, F32),
            shape_of((comps, XC), F32),
        ],
        in_specs=[SMEM] + [VMEM] * pieces + [ANY] * pieces + [VMEM] * 2,
        compiler_params=SMALL,
        out_specs=[VMEM] * 6,
        scratch_shapes=[pltpu.VMEM(footprints.shape, BF16), pltpu.VMEM(support.shape, F32)]
        + [pltpu.VMEM(part.shape, BF16) for part in all_traces]
        + movie_scratch,
    )(block_order, *all_traces, *movies, footprints, support)

    half, *joined = pl.pallas_call(
        functools.partial(footprint_kernel, pieces),
        out_shape=[shape_of((comps, share), BF16)]
        + [shape_of((comps, part.shape[1] + comps), F32) for part in movies],
        in_specs=[SMEM] + [VMEM] * 8 + [ANY] * pieces,
        compiler_params=SMALL,
        out_specs=[VMEM] * (pieces + 1),
        scratch_shapes=[pltpu.VMEM((comps, share), F32)] * 2 + [pltpu.VMEM((2 * comps, share), BF16)] + movie_scratch,
    )(block_order, target, keep, start, system, coef, scale, *sides, *movies)

    if cores == 2:
        ours, theirs = joined[0], swap(joined[1])
        other = swap(half)
        new_footprints = jnp.where(
            me == 0, jnp.concatenate([half, other], axis=1), jnp.concatenate([other, half], axis=1)
        )
    else:
        joined = joined[0]
        projection = lax.psum_scatter(joined[:, : frames * cores], "tm", scatter_dimension=1, tiled=True)
        ours = jnp.concatenate([projection, lax.psum(joined[:, frames * cores :], "tm")], axis=1)
        theirs = jnp.zeros_like(ours)
        new_footprints = lax.all_gather(half, "tm", axis=1, tiled=True)

    if planes == GROUP * GROUP:
        joined = sum_over_vox(ours, theirs)
    else:
        joined = [lax.psum(ours + theirs, "vox")]
    new_traces = pl.pallas_call(
        trace_kernel,
        out_shape=shape_of((comps, frames), F32),
        in_specs=[SMEM] + [VMEM] * (len(joined) + 1),
        compiler_params=SMALL,
        out_specs=VMEM,
        scratch_shapes=[
            pltpu.VMEM((comps, frames + comps), F32),
            pltpu.VMEM((comps, frames), F32),
            pltpu.VMEM((2 * comps, 2 * comps), BF16),
            pltpu.VMEM(table, F32),
            pltpu.VMEM((2 * comps, frames), BF16),
            pltpu.VMEM((comps, frames), F32),
        ],
    )(block_order, traces, *joined)
    return (new_footprints, new_traces)


def solution(mesh):
    placed = (P("vox", "tm"), P(None, "vox"), P(None, "tm"), P(None, "vox"), P())
    return jax.shard_map(
        local,
        mesh=mesh,
        in_specs=placed,
        out_specs=(P(None, "vox"), P(None, "tm")),
        check_vma=False,
    )
```

```python
import functools

import jax
import jax.numpy as jnp
from jax import lax
from jax.experimental import pallas as pl
from jax.experimental.pallas import tpu as pltpu
from jax.sharding import PartitionSpec as P

BLOCKC = 16
XC = 128
INNER = 3
GROUP = 4
RELAYED = 64

smooth_weight = 256.0
ridge_weight = 2048.0

F32 = jnp.float32
BF16 = jnp.bfloat16
VMEM = pl.BlockSpec(memory_space=pltpu.VMEM)
SMEM = pl.BlockSpec(memory_space=pltpu.SMEM)
ANY = pl.BlockSpec(memory_space=pl.ANY)
SMALL = pltpu.CompilerParams(vmem_limit_bytes=14 * 1024 * 1024)
BY_LAST = (((1,), (1,)), ((), ()))


def shape_of(dims, dtype):
    return jax.ShapeDtypeStruct(dims, dtype)


def split_terms(array):
    high = array.astype(BF16)
    return high, (array - high.astype(F32)).astype(BF16)


def rows_of(place):
    return slice(place * BLOCKC, (place + 1) * BLOCKC)


def rows_from(order_ref, place):
    return pl.ds(pl.multiple_of(order_ref[place] * BLOCKC, BLOCKC), BLOCKC)


def diagonal_of(gram):
    row = lax.broadcasted_iota(jnp.int32, gram.shape, 0)
    col = lax.broadcasted_iota(jnp.int32, gram.shape, 1)
    eye = row == col
    return eye, jnp.sum(jnp.where(eye, gram, 0.0), axis=1, keepdims=True)


def store_system(system, gs_ref, coef_ref):
    comps = system.shape[0]
    blocks = comps // BLOCKC
    high, low = split_terms(system)
    for place in range(blocks):
        rows = rows_of(place)
        before = (place - 1) % blocks * BLOCKC
        for side in range(2):
            lanes = slice(side * comps, (side + 1) * comps)
            gs_ref[rows_of(2 * place), lanes] = high[rows]
            gs_ref[rows_of(2 * place + 1), lanes] = low[rows]
        for k in range(BLOCKC):
            coef_ref[place, k] = jnp.broadcast_to(system[rows, before + k : before + k + 1], (BLOCKC, XC))


def sweep_steps(gs_ref, coef_ref, goal_ref, stacked_ref, value_ref, keep_ref=None, finished=None):
    comps, width = goal_ref.shape
    blocks = comps // BLOCKC

    def product_of(place):
        pair = slice(2 * BLOCKC * place, 2 * BLOCKC * (place + 1))
        product = jnp.dot(gs_ref[pair, :], stacked_ref[...], preferred_element_type=F32)
        return product[:BLOCKC] + product[BLOCKC:]

    steps = INNER * blocks
    ready, change = product_of(0), None
    for step in range(steps):
        place = step % blocks
        rows = rows_of(place)
        following = product_of((step + 1) % blocks) if step + 1 < steps else None
        base = goal_ref[rows, :] + ready
        columns = []
        for lane in range(0, width, XC):
            lanes = slice(lane, lane + XC)
            total = base[:, lanes]
            if change is not None:
                parts = [None] * 4
                for k in range(BLOCKC):
                    term = coef_ref[place, k] * jnp.broadcast_to(change[k : k + 1, lanes], (BLOCKC, XC))
                    parts[k % 4] = term if parts[k % 4] is None else parts[k % 4] + term
                total = total + ((parts[0] + parts[1]) + (parts[2] + parts[3]))
            columns.append(jnp.maximum(total, 0.0))
        updated = jnp.concatenate(columns, axis=1)
        if keep_ref is not None:
            updated = updated * keep_ref[rows, :]
        change = updated - value_ref[rows, :]
        value_ref[rows, :] = updated
        if finished is not None and step >= steps - blocks:
            finished(place)
        high, low = split_terms(updated)
        stacked_ref[rows, :] = high
        stacked_ref[comps + place * BLOCKC : comps + (place + 1) * BLOCKC, :] = low
        ready = following


def movie_rows(ref, share):
    if ref.shape[0] == share:
        return ref[...]
    return ref[pl.ds(pl.multiple_of(lax.axis_index("tm") * share, share), share), :]


def load_kernel(order_ref, fp_ref, support_ref, traces_ref, movie_ref, sorted_fp, support_out, sorted_traces, movie_own, sems):
    share = movie_own.shape[0]
    blocks = sorted_fp.shape[0] // BLOCKC
    mine = pl.ds(pl.multiple_of(lax.axis_index("tm") * share, share), share)
    pairs = [(movie_ref.at[mine, :], movie_own), (support_ref, support_out)]
    for place in range(blocks):
        rows, source = rows_of(place), rows_from(order_ref, place)
        pairs.append((fp_ref.at[source, :], sorted_fp.at[rows, :]))
        pairs.append((traces_ref.at[source, :], sorted_traces.at[rows, :]))
    copies = [pltpu.make_async_copy(source, target, sems.at[index]) for index, (source, target) in enumerate(pairs)]
    for copy in copies:
        copy.start()
    for copy in copies:
        copy.wait()


def smooth_kernel(order_ref, sorted_fp, support_buf, smooth_ref, keep_ref, start_ref, sorted_support):
    comps, share = smooth_ref.shape
    blocks = comps // BLOCKC
    spread = jnp.concatenate([support_buf[...].astype(F32)] * (XC // support_buf.shape[0]), axis=0).T
    sorted_support[comps:, :] = spread
    for place in range(blocks):
        source = pl.ds(pl.multiple_of(comps + order_ref[place] * BLOCKC, BLOCKC), BLOCKC)
        sorted_support[rows_of(place), :] = sorted_support[source, :]

    me = lax.axis_index("tm")
    count = sorted_fp.shape[1] // share
    first = me * share
    lane = lax.broadcasted_iota(jnp.int32, (comps, XC), 1)
    support = sorted_support[:comps, :]

    def row_at(offset):
        at = pl.multiple_of(first + offset, XC)
        return sorted_fp[:, pl.ds(at, XC)].astype(F32)

    below = pl.multiple_of(jnp.maximum(first - XC, 0), XC)
    above = pl.multiple_of(jnp.minimum(first + share, sorted_fp.shape[1] - XC), XC)
    before = sorted_fp[:, pl.ds(below, XC)].astype(F32) * jnp.where(me > 0, 1.0, 0.0)
    center = row_at(0)
    for offset in range(0, share, XC):
        if offset + XC < share:
            after = row_at(offset + XC)
        else:
            after = sorted_fp[:, pl.ds(above, XC)].astype(F32) * jnp.where(me < count - 1, 1.0, 0.0)
        left = jnp.where(lane == 0, 0.0, pltpu.roll(center, 1, 1))
        right = jnp.where(lane == XC - 1, 0.0, pltpu.roll(center, XC - 1, 1))
        beside = before + after + left + right
        lanes = slice(offset, offset + XC)
        smooth_ref[:, lanes] = smooth_weight * (6.0 * center - beside)
        here = me * (share // XC) + offset // XC
        kept = jnp.sum(jnp.where(lane == here, support, 0.0), axis=1, keepdims=True)
        kept = jnp.broadcast_to(kept, (comps, XC))
        keep_ref[:, lanes] = kept
        start_ref[:, lanes] = center * kept
        before, center = center, after


def target_kernel(pieces, smooth_ref, *refs):
    trace_refs, movie_refs, refs = refs[:pieces], refs[pieces : 2 * pieces], refs[2 * pieces :]
    target_ref, gs_ref, coef_ref, scale_ref = refs
    share = target_ref.shape[1]
    gram = None
    for ref in trace_refs:
        part = lax.dot_general(ref[...], ref[...], BY_LAST, preferred_element_type=F32)
        gram = part if gram is None else gram + part
    eye, diagonal = diagonal_of(gram)
    inverse = 1.0 / (diagonal + 6.0 * smooth_weight)
    store_system(jnp.where(eye, 6.0 * smooth_weight * inverse, -gram * inverse), gs_ref, coef_ref)
    scale_ref[...] = jnp.broadcast_to(smooth_weight * inverse, scale_ref.shape)
    correlation = None
    for ref, movie_ref in zip(trace_refs, movie_refs):
        part = lax.dot_general(ref[...], movie_rows(movie_ref, share), BY_LAST, preferred_element_type=F32)
        correlation = part if correlation is None else correlation + part
    target_ref[...] = (correlation - smooth_ref[...]) * inverse


def footprint_kernel(sides, order_ref, target_ref, keep_ref, start_ref, gs_ref, coef_ref, scale_ref, *refs):
    side_refs, refs = refs[:sides], refs[sides:]
    movie_ref, half_ref, sorted_ref, joined_ref, goal_ref, value_ref, stacked_ref, sides_ref = refs
    comps, share = target_ref.shape
    value_ref[...] = start_ref[...]
    stacked_ref[:comps, :] = start_ref[...].astype(BF16)
    stacked_ref[comps:, :] = jnp.zeros((comps, share), BF16)
    relayed = side_refs[0].shape[0]
    sides_ref[:relayed, :] = side_refs[0][...].astype(F32) + side_refs[1][...].astype(F32)
    sides_ref[relayed:, :] = side_refs[2][...].astype(F32) + side_refs[3][...].astype(F32)
    for place in range(comps // BLOCKC):
        rows, source = rows_of(place), rows_from(order_ref, place)
        for offset in range(0, share, XC):
            lanes = slice(offset, offset + XC)
            goal_ref[rows, lanes] = target_ref[rows, lanes] + sides_ref[source, lanes] * scale_ref[rows, :]
    sweep_steps(gs_ref, coef_ref, goal_ref, stacked_ref, value_ref, keep_ref)
    half = stacked_ref[:comps, :]
    sorted_ref[...] = half
    for place in range(comps // BLOCKC):
        half_ref[rows_from(order_ref, place), :] = stacked_ref[rows_of(place), :]
    store_products(half, movie_ref, joined_ref)


def store_products(half, movie_ref, joined_ref):
    frames = movie_ref.shape[1]
    joined_ref[:, :frames] = jnp.dot(half, movie_rows(movie_ref, half.shape[1]), preferred_element_type=F32)
    joined_ref[:, frames:] = lax.dot_general(half, half, BY_LAST, preferred_element_type=F32)


def product_kernel(half_ref, movie_ref, joined_ref):
    store_products(half_ref[...], movie_ref, joined_ref)


def chunk_kernel(stride, ours_ref, theirs_ref, *out_refs):
    rows = out_refs[0].shape[0]
    digit = lax.axis_index("vox") // stride % GROUP
    for index, out_ref in enumerate(out_refs):
        at = pl.ds(pl.multiple_of((digit ^ index) * rows, rows), rows)
        out_ref[...] = ours_ref[at, :] + theirs_ref[at, :]


def trace_kernel(order_ref, traces_ref, *refs):
    joined_refs, (out_ref, joined, goal_ref, gs_ref, coef_ref, stacked_ref, value_ref, sems) = refs[:-8], refs[-8:]
    comps, frames = traces_ref.shape
    digit = lax.axis_index("vox") % GROUP
    for index, ref in enumerate(joined_refs):
        rows = ref.shape[0]
        place = pl.multiple_of((digit ^ index) * rows, rows) if rows < comps else 0
        joined[pl.ds(place, rows), :] = ref[...]
    cross = joined[:, frames:]
    eye, diagonal = diagonal_of(cross)
    inverse = 1.0 / (diagonal + ridge_weight)
    store_system(jnp.where(eye, 0.0, -cross * inverse), gs_ref, coef_ref)
    goal_ref[...] = joined[:, :frames] * inverse
    stacked_ref[:comps, :] = traces_ref[...]
    value_ref[...] = traces_ref[...].astype(F32)
    stacked_ref[comps:, :] = jnp.zeros((comps, frames), BF16)
    copies = [
        pltpu.make_async_copy(value_ref.at[rows_of(place), :], out_ref.at[rows_from(order_ref, place), :], sems.at[place])
        for place in range(comps // BLOCKC)
    ]
    sweep_steps(gs_ref, coef_ref, goal_ref, stacked_ref, value_ref, None, lambda place: copies[place].start())
    for copy in copies:
        copy.wait()


def in_hbm(array):
    return pltpu.with_memory_space_constraint(array, pltpu.HBM)


def swap(array):
    return lax.ppermute(array, "tm", [(0, 1), (1, 0)])


def from_group(arrays, stride):
    count = lax.axis_size("vox")
    return [lax.ppermute(array, "vox", [(i, i ^ (k * stride)) for i in range(count)]) for k, array in arrays]


def tree_sum(own, others):
    return (own + others[0]) + (others[1] + others[2])


def sum_over_vox(ours, theirs):
    comps, width = ours.shape
    rows = comps // GROUP
    top = lax.axis_size("vox") // GROUP
    chunks = pl.pallas_call(
        functools.partial(chunk_kernel, 1),
        out_shape=[shape_of((rows, width), F32)] * GROUP,
        in_specs=[VMEM] * 2,
        compiler_params=SMALL,
        out_specs=[VMEM] * GROUP,
    )(ours, theirs)
    mine = tree_sum(chunks[0], from_group([(k, chunks[k]) for k in range(1, GROUP)], 1))
    mine = tree_sum(mine, from_group([(k, mine) for k in range(1, GROUP)], top))
    return [mine] + from_group([(k, mine) for k in range(1, GROUP)], 1)


def local(movie, footprints, traces, support, block_order):
    comps, vox_local = footprints.shape
    frames = traces.shape[1]
    cores = lax.axis_size("tm")
    planes = lax.axis_size("vox")
    share = vox_local // cores
    me = lax.axis_index("tm")

    own = lax.dynamic_slice_in_dim(footprints, me * share, share, 1)
    pairs = [(i, i ^ 1) for i in range(planes)]
    across = [(i, i + 1) for i in range(1, planes - 1, 2)] + [(i + 1, i) for i in range(1, planes - 1, 2)]
    onward = [(i, i + 2) for i in range(0, planes - 2, 2)] + [(i, i - 2) for i in range(3, planes, 2)]
    relayed, direct = lax.optimization_barrier((own[:RELAYED], own[RELAYED:]))
    beside_relayed = lax.ppermute(relayed, "vox", pairs)
    across_direct = lax.ppermute(direct, "vox", across)
    beside_direct = lax.ppermute(direct, "vox", pairs)
    blocks = comps // BLOCKC
    sorted_fp, support_rows, sorted_traces, movie_own = pl.pallas_call(
        load_kernel,
        out_shape=[
            shape_of(footprints.shape, BF16),
            shape_of(support.shape[::-1], jnp.int32),
            shape_of(traces.shape, BF16),
            shape_of((share, frames), BF16),
        ],
        in_specs=[SMEM] + [ANY] * 4,
        compiler_params=SMALL,
        out_specs=[VMEM] * 4,
        scratch_shapes=[pltpu.SemaphoreType.DMA((2 * blocks + 2,))],
    )(*[in_hbm(array) for array in (block_order, footprints, support.T, traces, movie)])
    sides = [beside_relayed, lax.ppermute(beside_relayed, "vox", onward), beside_direct, across_direct]

    smooth, keep, start = pl.pallas_call(
        smooth_kernel,
        out_shape=[shape_of((comps, share), F32)] * 3,
        in_specs=[SMEM] + [VMEM] * 2,
        compiler_params=SMALL,
        out_specs=[VMEM] * 3,
        scratch_shapes=[pltpu.VMEM((2 * comps, XC), F32)],
    )(in_hbm(block_order), sorted_fp, support_rows)

    if cores == 2:
        movies = [movie_own, swap(movie)]
        all_traces = [sorted_traces, swap(sorted_traces)]
    else:
        movies = [lax.all_to_all(movie, "tm", 0, 1, tiled=True)]
        all_traces = [lax.all_gather(sorted_traces, "tm", axis=1, tiled=True)]
    pieces = len(movies)
    table = (blocks, BLOCKC, BLOCKC, XC)
    target, system, coef, scale = pl.pallas_call(
        functools.partial(target_kernel, pieces),
        out_shape=[
            shape_of((comps, share), F32),
            shape_of((2 * comps, 2 * comps), BF16),
            shape_of(table, F32),
            shape_of((comps, XC), F32),
        ],
        in_specs=[VMEM] * (2 * pieces + 1),
        compiler_params=SMALL,
        out_specs=[VMEM] * 4,
    )(smooth, *all_traces, *movies)

    half, sorted_half, joined = pl.pallas_call(
        functools.partial(footprint_kernel, len(sides)),
        out_shape=[shape_of((comps, share), BF16)] * 2 + [shape_of((comps, movies[-1].shape[1] + comps), F32)],
        in_specs=[SMEM] + [VMEM] * (7 + len(sides)),
        compiler_params=SMALL,
        out_specs=[VMEM] * 3,
        scratch_shapes=[pltpu.VMEM((comps, share), F32)] * 2
        + [pltpu.VMEM((2 * comps, share), BF16), pltpu.VMEM((comps, share), F32)],
    )(block_order, target, keep, start, system, coef, scale, *sides, movies[-1])

    if cores == 2:
        theirs = swap(joined)
        ours = pl.pallas_call(
            product_kernel,
            out_shape=shape_of((comps, frames + comps), F32),
            in_specs=[VMEM] * 2,
            compiler_params=SMALL,
            out_specs=VMEM,
        )(sorted_half, movies[0])
        other = swap(half)
        new_footprints = jnp.where(
            me == 0, jnp.concatenate([half, other], axis=1), jnp.concatenate([other, half], axis=1)
        )
    else:
        projection = lax.psum_scatter(joined[:, : frames * cores], "tm", scatter_dimension=1, tiled=True)
        ours = jnp.concatenate([projection, lax.psum(joined[:, frames * cores :], "tm")], axis=1)
        theirs = jnp.zeros_like(ours)
        new_footprints = lax.all_gather(half, "tm", axis=1, tiled=True)

    if planes == GROUP * GROUP:
        joined = sum_over_vox(ours, theirs)
    else:
        joined = [lax.psum(ours + theirs, "vox")]
    new_traces = pl.pallas_call(
        trace_kernel,
        out_shape=shape_of((comps, frames), F32),
        in_specs=[SMEM] + [VMEM] * (len(joined) + 1),
        compiler_params=SMALL,
        out_specs=ANY,
        scratch_shapes=[
            pltpu.VMEM((comps, frames + comps), F32),
            pltpu.VMEM((comps, frames), F32),
            pltpu.VMEM((2 * comps, 2 * comps), BF16),
            pltpu.VMEM(table, F32),
            pltpu.VMEM((2 * comps, frames), BF16),
            pltpu.VMEM((comps, frames), F32),
            pltpu.SemaphoreType.DMA((blocks,)),
        ],
    )(block_order, sorted_traces, *joined)
    return (new_footprints, new_traces)


def solution(mesh):
    placed = (P("vox", "tm"), P(None, "vox"), P(None, "tm"), P(None, "vox"), P())
    return jax.shard_map(
        local,
        mesh=mesh,
        in_specs=placed,
        out_specs=(P(None, "vox"), P(None, "tm")),
        check_vma=False,
    )
```

```python
import functools

import jax
import jax.numpy as jnp
from jax import lax
from jax.experimental import pallas as pl
from jax.experimental.pallas import tpu as pltpu
from jax.sharding import PartitionSpec as P

BLOCKC = 16
XC = 128
INNER = 3
GROUP = 4
RELAYED = 64

smooth_weight = 256.0
ridge_weight = 2048.0

F32 = jnp.float32
BF16 = jnp.bfloat16
VMEM = pl.BlockSpec(memory_space=pltpu.VMEM)
SMEM = pl.BlockSpec(memory_space=pltpu.SMEM)
ANY = pl.BlockSpec(memory_space=pl.ANY)
SMALL = pltpu.CompilerParams(vmem_limit_bytes=14 * 1024 * 1024)
BY_LAST = (((1,), (1,)), ((), ()))


def shape_of(dims, dtype):
    return jax.ShapeDtypeStruct(dims, dtype)


def split_terms(array):
    high = array.astype(BF16)
    return high, (array - high.astype(F32)).astype(BF16)


def rows_of(place):
    return slice(place * BLOCKC, (place + 1) * BLOCKC)


def rows_from(order_ref, place):
    return pl.ds(pl.multiple_of(order_ref[place] * BLOCKC, BLOCKC), BLOCKC)


def diagonal_of(gram):
    row = lax.broadcasted_iota(jnp.int32, gram.shape, 0)
    col = lax.broadcasted_iota(jnp.int32, gram.shape, 1)
    eye = row == col
    return eye, jnp.sum(jnp.where(eye, gram, 0.0), axis=1, keepdims=True)


def store_system(system, gs_ref, coef_ref):
    comps = system.shape[0]
    blocks = comps // BLOCKC
    high, low = split_terms(system)
    for place in range(blocks):
        rows = rows_of(place)
        before = (place - 1) % blocks * BLOCKC
        for side in range(2):
            lanes = slice(side * comps, (side + 1) * comps)
            gs_ref[rows_of(2 * place), lanes] = high[rows]
            gs_ref[rows_of(2 * place + 1), lanes] = low[rows]
        for k in range(BLOCKC):
            coef_ref[place, k] = jnp.broadcast_to(system[rows, before + k : before + k + 1], (BLOCKC, XC))


def sweep_steps(gs_ref, coef_ref, goal_ref, stacked_ref, value_ref, keep_ref=None, finished=None):
    comps, width = goal_ref.shape
    blocks = comps // BLOCKC

    def product_of(place):
        pair = slice(2 * BLOCKC * place, 2 * BLOCKC * (place + 1))
        product = jnp.dot(gs_ref[pair, :], stacked_ref[...], preferred_element_type=F32)
        return product[:BLOCKC] + product[BLOCKC:]

    steps = INNER * blocks
    ready, change = product_of(0), None
    for step in range(steps):
        place = step % blocks
        rows = rows_of(place)
        following = product_of((step + 1) % blocks) if step + 1 < steps else None
        base = goal_ref[rows, :] + ready
        columns = []
        for lane in range(0, width, XC):
            lanes = slice(lane, lane + XC)
            total = base[:, lanes]
            if change is not None:
                parts = [None] * 4
                for k in range(BLOCKC):
                    term = coef_ref[place, k] * jnp.broadcast_to(change[k : k + 1, lanes], (BLOCKC, XC))
                    parts[k % 4] = term if parts[k % 4] is None else parts[k % 4] + term
                total = total + ((parts[0] + parts[1]) + (parts[2] + parts[3]))
            columns.append(jnp.maximum(total, 0.0))
        updated = jnp.concatenate(columns, axis=1)
        if keep_ref is not None:
            updated = updated * keep_ref[rows, :]
        change = updated - value_ref[rows, :]
        value_ref[rows, :] = updated
        if finished is not None and step >= steps - blocks:
            finished(place)
        high, low = split_terms(updated)
        stacked_ref[rows, :] = high
        stacked_ref[comps + place * BLOCKC : comps + (place + 1) * BLOCKC, :] = low
        ready = following


def movie_rows(ref, share):
    if ref.shape[0] == share:
        return ref[...]
    return ref[pl.ds(pl.multiple_of(lax.axis_index("tm") * share, share), share), :]


def load_kernel(order_hbm, fp_ref, support_ref, traces_ref, movie_ref, relayed, direct, sorted_fp, support_out, sorted_traces, movie_own, order_ref, sems):
    share = movie_own.shape[0]
    cut = relayed.shape[0]
    blocks = sorted_fp.shape[0] // BLOCKC
    mine = pl.ds(pl.multiple_of(lax.axis_index("tm") * share, share), share)
    order_copy = pltpu.make_async_copy(order_hbm, order_ref, sems.at[0])
    order_copy.start()
    pairs = [
        (fp_ref.at[:cut, mine], relayed),
        (fp_ref.at[cut:, mine], direct),
        (support_ref, support_out),
        (movie_ref.at[mine, :], movie_own),
    ]
    copies = [pltpu.make_async_copy(source, target, sems.at[1 + index]) for index, (source, target) in enumerate(pairs)]
    for copy in copies:
        copy.start()
    order_copy.wait()
    pairs = []
    for place in range(blocks):
        rows, source = rows_of(place), rows_from(order_ref, place)
        pairs.append((fp_ref.at[source, :], sorted_fp.at[rows, :]))
        pairs.append((traces_ref.at[source, :], sorted_traces.at[rows, :]))
    later = [pltpu.make_async_copy(source, target, sems.at[5 + index]) for index, (source, target) in enumerate(pairs)]
    for copy in later:
        copy.start()
    for copy in copies + later:
        copy.wait()


def smooth_kernel(order_ref, sorted_fp, support_buf, smooth_ref, keep_ref, start_ref, sorted_support):
    comps, share = smooth_ref.shape
    blocks = comps // BLOCKC
    spread = jnp.concatenate([support_buf[...].astype(F32)] * (XC // support_buf.shape[0]), axis=0).T
    sorted_support[comps:, :] = spread
    for place in range(blocks):
        source = pl.ds(pl.multiple_of(comps + order_ref[place] * BLOCKC, BLOCKC), BLOCKC)
        sorted_support[rows_of(place), :] = sorted_support[source, :]

    me = lax.axis_index("tm")
    count = sorted_fp.shape[1] // share
    first = me * share
    lane = lax.broadcasted_iota(jnp.int32, (comps, XC), 1)
    support = sorted_support[:comps, :]

    def row_at(offset):
        at = pl.multiple_of(first + offset, XC)
        return sorted_fp[:, pl.ds(at, XC)].astype(F32)

    below = pl.multiple_of(jnp.maximum(first - XC, 0), XC)
    above = pl.multiple_of(jnp.minimum(first + share, sorted_fp.shape[1] - XC), XC)
    before = sorted_fp[:, pl.ds(below, XC)].astype(F32) * jnp.where(me > 0, 1.0, 0.0)
    center = row_at(0)
    for offset in range(0, share, XC):
        if offset + XC < share:
            after = row_at(offset + XC)
        else:
            after = sorted_fp[:, pl.ds(above, XC)].astype(F32) * jnp.where(me < count - 1, 1.0, 0.0)
        left = jnp.where(lane == 0, 0.0, pltpu.roll(center, 1, 1))
        right = jnp.where(lane == XC - 1, 0.0, pltpu.roll(center, XC - 1, 1))
        beside = before + after + left + right
        lanes = slice(offset, offset + XC)
        smooth_ref[:, lanes] = smooth_weight * (6.0 * center - beside)
        here = me * (share // XC) + offset // XC
        kept = jnp.sum(jnp.where(lane == here, support, 0.0), axis=1, keepdims=True)
        kept = jnp.broadcast_to(kept, (comps, XC))
        keep_ref[:, lanes] = kept
        start_ref[:, lanes] = center * kept
        before, center = center, after


def target_kernel(pieces, smooth_ref, *refs):
    trace_refs, movie_refs, refs = refs[:pieces], refs[pieces : 2 * pieces], refs[2 * pieces :]
    target_ref, gs_ref, coef_ref, scale_ref = refs
    share = target_ref.shape[1]
    gram = None
    for ref in trace_refs:
        part = lax.dot_general(ref[...], ref[...], BY_LAST, preferred_element_type=F32)
        gram = part if gram is None else gram + part
    eye, diagonal = diagonal_of(gram)
    inverse = 1.0 / (diagonal + 6.0 * smooth_weight)
    store_system(jnp.where(eye, 6.0 * smooth_weight * inverse, -gram * inverse), gs_ref, coef_ref)
    scale_ref[...] = jnp.broadcast_to(smooth_weight * inverse, scale_ref.shape)
    correlation = None
    for ref, movie_ref in zip(trace_refs, movie_refs):
        part = lax.dot_general(ref[...], movie_rows(movie_ref, share), BY_LAST, preferred_element_type=F32)
        correlation = part if correlation is None else correlation + part
    target_ref[...] = (correlation - smooth_ref[...]) * inverse


def footprint_kernel(sides, order_ref, target_ref, keep_ref, start_ref, gs_ref, coef_ref, scale_ref, *refs):
    side_refs, refs = refs[:sides], refs[sides:]
    movie_ref, half_ref, sorted_ref, joined_ref, goal_ref, value_ref, stacked_ref, sides_ref = refs
    comps, share = target_ref.shape
    value_ref[...] = start_ref[...]
    stacked_ref[:comps, :] = start_ref[...].astype(BF16)
    stacked_ref[comps:, :] = jnp.zeros((comps, share), BF16)
    relayed = side_refs[0].shape[0]
    sides_ref[:relayed, :] = side_refs[0][...].astype(F32) + side_refs[1][...].astype(F32)
    sides_ref[relayed:, :] = side_refs[2][...].astype(F32) + side_refs[3][...].astype(F32)
    for place in range(comps // BLOCKC):
        rows, source = rows_of(place), rows_from(order_ref, place)
        for offset in range(0, share, XC):
            lanes = slice(offset, offset + XC)
            goal_ref[rows, lanes] = target_ref[rows, lanes] + sides_ref[source, lanes] * scale_ref[rows, :]
    sweep_steps(gs_ref, coef_ref, goal_ref, stacked_ref, value_ref, keep_ref)
    half = stacked_ref[:comps, :]
    sorted_ref[...] = half
    for place in range(comps // BLOCKC):
        half_ref[rows_from(order_ref, place), :] = stacked_ref[rows_of(place), :]
    store_products(half, movie_ref, joined_ref)


def store_products(half, movie_ref, joined_ref):
    frames = movie_ref.shape[1]
    joined_ref[:, :frames] = jnp.dot(half, movie_rows(movie_ref, half.shape[1]), preferred_element_type=F32)
    joined_ref[:, frames:] = lax.dot_general(half, half, BY_LAST, preferred_element_type=F32)


def product_kernel(half_ref, movie_ref, joined_ref):
    store_products(half_ref[...], movie_ref, joined_ref)


def chunk_kernel(stride, ours_ref, theirs_ref, *out_refs):
    rows = out_refs[0].shape[0]
    digit = lax.axis_index("vox") // stride % GROUP
    for index, out_ref in enumerate(out_refs):
        at = pl.ds(pl.multiple_of((digit ^ index) * rows, rows), rows)
        out_ref[...] = ours_ref[at, :] + theirs_ref[at, :]


def trace_kernel(order_ref, traces_ref, *refs):
    joined_refs, (out_ref, joined, goal_ref, gs_ref, coef_ref, stacked_ref, value_ref, sems) = refs[:-8], refs[-8:]
    comps, frames = traces_ref.shape
    digit = lax.axis_index("vox") % GROUP
    for index, ref in enumerate(joined_refs):
        rows = ref.shape[0]
        step = (GROUP - index) % GROUP
        place = pl.multiple_of((digit ^ step) * rows, rows) if rows < comps else 0
        joined[pl.ds(place, rows), :] = ref[...]
    cross = joined[:, frames:]
    eye, diagonal = diagonal_of(cross)
    inverse = 1.0 / (diagonal + ridge_weight)
    store_system(jnp.where(eye, 0.0, -cross * inverse), gs_ref, coef_ref)
    goal_ref[...] = joined[:, :frames] * inverse
    stacked_ref[:comps, :] = traces_ref[...]
    value_ref[...] = traces_ref[...].astype(F32)
    stacked_ref[comps:, :] = jnp.zeros((comps, frames), BF16)
    copies = [
        pltpu.make_async_copy(value_ref.at[rows_of(place), :], out_ref.at[rows_from(order_ref, place), :], sems.at[place])
        for place in range(comps // BLOCKC)
    ]
    sweep_steps(gs_ref, coef_ref, goal_ref, stacked_ref, value_ref, None, lambda place: copies[place].start())
    for copy in copies:
        copy.wait()


def in_hbm(array):
    return pltpu.with_memory_space_constraint(array, pltpu.HBM)


def swap(array):
    return lax.ppermute(array, "tm", [(0, 1), (1, 0)])


def from_group(arrays, stride):
    count = lax.axis_size("vox")
    return [lax.ppermute(array, "vox", [(i, i ^ (k * stride)) for i in range(count)]) for k, array in arrays]


def tree_sum(own, others):
    return (others[1] + others[2]) + (own + others[0])


def sum_over_vox(ours, theirs):
    comps, width = ours.shape
    rows = comps // GROUP
    top = lax.axis_size("vox") // GROUP
    chunks = pl.pallas_call(
        functools.partial(chunk_kernel, 1),
        out_shape=[shape_of((rows, width), F32)] * GROUP,
        in_specs=[VMEM] * 2,
        compiler_params=SMALL,
        out_specs=[VMEM] * GROUP,
    )(ours, theirs)
    mine = tree_sum(chunks[0], from_group([(k, chunks[k]) for k in range(1, GROUP)], 1))
    mine = tree_sum(mine, from_group([(k, mine) for k in range(1, GROUP)], top))
    return [mine] + from_group([(k, mine) for k in range(1, GROUP)], 1)[::-1]


def local(movie, footprints, traces, support, block_order):
    comps, vox_local = footprints.shape
    frames = traces.shape[1]
    cores = lax.axis_size("tm")
    planes = lax.axis_size("vox")
    share = vox_local // cores
    me = lax.axis_index("tm")

    pairs = [(i, i ^ 1) for i in range(planes)]
    across = [(i, i + 1) for i in range(1, planes - 1, 2)] + [(i + 1, i) for i in range(1, planes - 1, 2)]
    onward = [(i, i + 2) for i in range(0, planes - 2, 2)] + [(i, i - 2) for i in range(3, planes, 2)]
    blocks = comps // BLOCKC
    relayed, direct, sorted_fp, support_rows, sorted_traces, movie_own = pl.pallas_call(
        load_kernel,
        out_shape=[
            shape_of((RELAYED, share), BF16),
            shape_of((comps - RELAYED, share), BF16),
            shape_of(footprints.shape, BF16),
            shape_of(support.shape[::-1], jnp.int32),
            shape_of(traces.shape, BF16),
            shape_of((share, frames), BF16),
        ],
        in_specs=[ANY] * 5,
        compiler_params=SMALL,
        out_specs=[VMEM] * 6,
        scratch_shapes=[pltpu.SMEM(block_order.shape, jnp.int32), pltpu.SemaphoreType.DMA((2 * blocks + 5,))],
    )(*[in_hbm(array) for array in (block_order, footprints, support.T, traces, movie)])
    beside_relayed = lax.ppermute(relayed, "vox", pairs)
    across_direct = lax.ppermute(direct, "vox", across)
    beside_direct = lax.ppermute(direct, "vox", pairs)
    sides = [beside_relayed, lax.ppermute(beside_relayed, "vox", onward), beside_direct, across_direct]

    smooth, keep, start = pl.pallas_call(
        smooth_kernel,
        out_shape=[shape_of((comps, share), F32)] * 3,
        in_specs=[SMEM] + [VMEM] * 2,
        compiler_params=SMALL,
        out_specs=[VMEM] * 3,
        scratch_shapes=[pltpu.VMEM((2 * comps, XC), F32)],
    )(in_hbm(block_order), sorted_fp, support_rows)

    if cores == 2:
        movies = [movie_own, swap(movie)]
        all_traces = [sorted_traces, swap(sorted_traces)]
    else:
        movies = [lax.all_to_all(movie, "tm", 0, 1, tiled=True)]
        all_traces = [lax.all_gather(sorted_traces, "tm", axis=1, tiled=True)]
    pieces = len(movies)
    table = (blocks, BLOCKC, BLOCKC, XC)
    target, system, coef, scale = pl.pallas_call(
        functools.partial(target_kernel, pieces),
        out_shape=[
            shape_of((comps, share), F32),
            shape_of((2 * comps, 2 * comps), BF16),
            shape_of(table, F32),
            shape_of((comps, XC), F32),
        ],
        in_specs=[VMEM] * (2 * pieces + 1),
        compiler_params=SMALL,
        out_specs=[VMEM] * 4,
    )(smooth, *all_traces, *movies)

    half, sorted_half, joined = pl.pallas_call(
        functools.partial(footprint_kernel, len(sides)),
        out_shape=[shape_of((comps, share), BF16)] * 2 + [shape_of((comps, movies[-1].shape[1] + comps), F32)],
        in_specs=[SMEM] + [VMEM] * (7 + len(sides)),
        compiler_params=SMALL,
        out_specs=[VMEM] * 3,
        scratch_shapes=[pltpu.VMEM((comps, share), F32)] * 2
        + [pltpu.VMEM((2 * comps, share), BF16), pltpu.VMEM((comps, share), F32)],
    )(block_order, target, keep, start, system, coef, scale, *sides, movies[-1])

    if cores == 2:
        theirs = swap(joined)
        ours = pl.pallas_call(
            product_kernel,
            out_shape=shape_of((comps, frames + comps), F32),
            in_specs=[VMEM] * 2,
            compiler_params=SMALL,
            out_specs=VMEM,
        )(sorted_half, movies[0])
        other = swap(half)
        new_footprints = jnp.where(
            me == 0, jnp.concatenate([half, other], axis=1), jnp.concatenate([other, half], axis=1)
        )
    else:
        projection = lax.psum_scatter(joined[:, : frames * cores], "tm", scatter_dimension=1, tiled=True)
        ours = jnp.concatenate([projection, lax.psum(joined[:, frames * cores :], "tm")], axis=1)
        theirs = jnp.zeros_like(ours)
        new_footprints = lax.all_gather(half, "tm", axis=1, tiled=True)

    if planes == GROUP * GROUP:
        joined = sum_over_vox(ours, theirs)
    else:
        joined = [lax.psum(ours + theirs, "vox")]
    new_traces = pl.pallas_call(
        trace_kernel,
        out_shape=shape_of((comps, frames), F32),
        in_specs=[SMEM] + [VMEM] * (len(joined) + 1),
        compiler_params=SMALL,
        out_specs=ANY,
        scratch_shapes=[
            pltpu.VMEM((comps, frames + comps), F32),
            pltpu.VMEM((comps, frames), F32),
            pltpu.VMEM((2 * comps, 2 * comps), BF16),
            pltpu.VMEM(table, F32),
            pltpu.VMEM((2 * comps, frames), BF16),
            pltpu.VMEM((comps, frames), F32),
            pltpu.SemaphoreType.DMA((blocks,)),
        ],
    )(block_order, sorted_traces, *joined)
    return (new_footprints, new_traces)


def solution(mesh):
    placed = (P("vox", "tm"), P(None, "vox"), P(None, "tm"), P(None, "vox"), P())
    return jax.shard_map(
        local,
        mesh=mesh,
        in_specs=placed,
        out_specs=(P(None, "vox"), P(None, "tm")),
        check_vma=False,
    )
```

```python
import functools

import jax
import jax.numpy as jnp
from jax import lax
from jax.experimental import pallas as pl
from jax.experimental.pallas import tpu as pltpu
from jax.sharding import PartitionSpec as P

BLOCKC = 16
XC = 128
INNER = 3
GROUP = 4
RELAYED = 64

smooth_weight = 256.0
ridge_weight = 2048.0

F32 = jnp.float32
BF16 = jnp.bfloat16
VMEM = pl.BlockSpec(memory_space=pltpu.VMEM)
SMEM = pl.BlockSpec(memory_space=pltpu.SMEM)
ANY = pl.BlockSpec(memory_space=pl.ANY)
SMALL = pltpu.CompilerParams(vmem_limit_bytes=14 * 1024 * 1024)
BY_LAST = (((1,), (1,)), ((), ()))


def shape_of(dims, dtype):
    return jax.ShapeDtypeStruct(dims, dtype)


def split_terms(array):
    high = array.astype(BF16)
    return high, (array - high.astype(F32)).astype(BF16)


def rows_of(place):
    return slice(place * BLOCKC, (place + 1) * BLOCKC)


def rows_from(order_ref, place):
    return pl.ds(pl.multiple_of(order_ref[place] * BLOCKC, BLOCKC), BLOCKC)


def diagonal_of(gram):
    row = lax.broadcasted_iota(jnp.int32, gram.shape, 0)
    col = lax.broadcasted_iota(jnp.int32, gram.shape, 1)
    eye = row == col
    return eye, jnp.sum(jnp.where(eye, gram, 0.0), axis=1, keepdims=True)


def store_system(system, gs_ref, coef_ref):
    comps = system.shape[0]
    blocks = comps // BLOCKC
    high, low = split_terms(system)
    for place in range(blocks):
        rows = rows_of(place)
        before = (place - 1) % blocks * BLOCKC
        for side in range(2):
            lanes = slice(side * comps, (side + 1) * comps)
            gs_ref[rows_of(2 * place), lanes] = high[rows]
            gs_ref[rows_of(2 * place + 1), lanes] = low[rows]
        for k in range(BLOCKC):
            coef_ref[place, k] = jnp.broadcast_to(system[rows, before + k : before + k + 1], (BLOCKC, XC))


def sweep_steps(gs_ref, coef_ref, goal_ref, stacked_ref, value_ref, keep_ref=None, finished=None):
    comps, width = goal_ref.shape
    blocks = comps // BLOCKC

    def product_of(place):
        pair = slice(2 * BLOCKC * place, 2 * BLOCKC * (place + 1))
        product = jnp.dot(gs_ref[pair, :], stacked_ref[...], preferred_element_type=F32)
        return product[:BLOCKC] + product[BLOCKC:]

    steps = INNER * blocks
    ready, change = product_of(0), None
    for step in range(steps):
        place = step % blocks
        rows = rows_of(place)
        following = product_of((step + 1) % blocks) if step + 1 < steps else None
        base = goal_ref[rows, :] + ready
        columns = []
        for lane in range(0, width, XC):
            lanes = slice(lane, lane + XC)
            total = base[:, lanes]
            if change is not None:
                parts = [None] * 4
                for k in range(BLOCKC):
                    term = coef_ref[place, k] * jnp.broadcast_to(change[k : k + 1, lanes], (BLOCKC, XC))
                    parts[k % 4] = term if parts[k % 4] is None else parts[k % 4] + term
                total = total + ((parts[0] + parts[1]) + (parts[2] + parts[3]))
            columns.append(jnp.maximum(total, 0.0))
        updated = jnp.concatenate(columns, axis=1)
        if keep_ref is not None:
            updated = updated * keep_ref[rows, :]
        change = updated - value_ref[rows, :]
        value_ref[rows, :] = updated
        if finished is not None and step >= steps - blocks:
            finished(place)
        high, low = split_terms(updated)
        stacked_ref[rows, :] = high
        stacked_ref[comps + place * BLOCKC : comps + (place + 1) * BLOCKC, :] = low
        ready = following


def movie_rows(ref, share):
    if ref.shape[0] == share:
        return ref[...]
    return ref[pl.ds(pl.multiple_of(lax.axis_index("tm") * share, share), share), :]


def load_kernel(order_hbm, fp_ref, support_ref, traces_ref, movie_ref, relayed, direct, sorted_fp, support_out, sorted_traces, movie_own, order_ref, sems):
    share = movie_own.shape[0]
    cut = relayed.shape[0]
    blocks = sorted_fp.shape[0] // BLOCKC
    mine = pl.ds(pl.multiple_of(lax.axis_index("tm") * share, share), share)
    order_copy = pltpu.make_async_copy(order_hbm, order_ref, sems.at[0])
    order_copy.start()
    pairs = [
        (fp_ref.at[:cut, mine], relayed),
        (fp_ref.at[cut:, mine], direct),
        (support_ref, support_out),
        (movie_ref.at[mine, :], movie_own),
    ]
    copies = [pltpu.make_async_copy(source, target, sems.at[1 + index]) for index, (source, target) in enumerate(pairs)]
    for copy in copies:
        copy.start()
    order_copy.wait()
    pairs = []
    for place in range(blocks):
        rows, source = rows_of(place), rows_from(order_ref, place)
        pairs.append((fp_ref.at[source, :], sorted_fp.at[rows, :]))
        pairs.append((traces_ref.at[source, :], sorted_traces.at[rows, :]))
    later = [pltpu.make_async_copy(source, target, sems.at[5 + index]) for index, (source, target) in enumerate(pairs)]
    for copy in later:
        copy.start()
    for copy in copies + later:
        copy.wait()


def smooth_kernel(order_ref, sorted_fp, support_buf, smooth_ref, keep_ref, start_ref, sorted_support):
    comps, share = smooth_ref.shape
    blocks = comps // BLOCKC
    spread = jnp.concatenate([support_buf[...].astype(F32)] * (XC // support_buf.shape[0]), axis=0).T
    sorted_support[comps:, :] = spread
    for place in range(blocks):
        source = pl.ds(pl.multiple_of(comps + order_ref[place] * BLOCKC, BLOCKC), BLOCKC)
        sorted_support[rows_of(place), :] = sorted_support[source, :]

    me = lax.axis_index("tm")
    count = sorted_fp.shape[1] // share
    first = me * share
    lane = lax.broadcasted_iota(jnp.int32, (comps, XC), 1)
    support = sorted_support[:comps, :]

    def row_at(offset):
        at = pl.multiple_of(first + offset, XC)
        return sorted_fp[:, pl.ds(at, XC)].astype(F32)

    below = pl.multiple_of(jnp.maximum(first - XC, 0), XC)
    above = pl.multiple_of(jnp.minimum(first + share, sorted_fp.shape[1] - XC), XC)
    before = sorted_fp[:, pl.ds(below, XC)].astype(F32) * jnp.where(me > 0, 1.0, 0.0)
    center = row_at(0)
    for offset in range(0, share, XC):
        if offset + XC < share:
            after = row_at(offset + XC)
        else:
            after = sorted_fp[:, pl.ds(above, XC)].astype(F32) * jnp.where(me < count - 1, 1.0, 0.0)
        left = jnp.where(lane == 0, 0.0, pltpu.roll(center, 1, 1))
        right = jnp.where(lane == XC - 1, 0.0, pltpu.roll(center, XC - 1, 1))
        beside = before + after + left + right
        lanes = slice(offset, offset + XC)
        smooth_ref[:, lanes] = smooth_weight * (6.0 * center - beside)
        here = me * (share // XC) + offset // XC
        kept = jnp.sum(jnp.where(lane == here, support, 0.0), axis=1, keepdims=True)
        kept = jnp.broadcast_to(kept, (comps, XC))
        keep_ref[:, lanes] = kept
        start_ref[:, lanes] = center * kept
        before, center = center, after


def target_kernel(pieces, smooth_ref, *refs):
    trace_refs, movie_refs, refs = refs[:pieces], refs[pieces : 2 * pieces], refs[2 * pieces :]
    target_ref, gs_ref, coef_ref, scale_ref = refs
    share = target_ref.shape[1]
    gram = None
    for ref in trace_refs:
        part = lax.dot_general(ref[...], ref[...], BY_LAST, preferred_element_type=F32)
        gram = part if gram is None else gram + part
    eye, diagonal = diagonal_of(gram)
    inverse = 1.0 / (diagonal + 6.0 * smooth_weight)
    store_system(jnp.where(eye, 6.0 * smooth_weight * inverse, -gram * inverse), gs_ref, coef_ref)
    scale_ref[...] = jnp.broadcast_to(smooth_weight * inverse, scale_ref.shape)
    correlation = None
    for ref, movie_ref in zip(trace_refs, movie_refs):
        part = lax.dot_general(ref[...], movie_rows(movie_ref, share), BY_LAST, preferred_element_type=F32)
        correlation = part if correlation is None else correlation + part
    target_ref[...] = (correlation - smooth_ref[...]) * inverse


def footprint_kernel(sides, order_ref, target_ref, keep_ref, start_ref, gs_ref, coef_ref, scale_ref, *refs):
    side_refs, refs = refs[:sides], refs[sides:]
    movie_ref, half_ref, sorted_ref, joined_ref, goal_ref, value_ref, stacked_ref, sides_ref = refs
    comps, share = target_ref.shape
    value_ref[...] = start_ref[...]
    stacked_ref[:comps, :] = start_ref[...].astype(BF16)
    stacked_ref[comps:, :] = jnp.zeros((comps, share), BF16)
    relayed = side_refs[0].shape[0]
    sides_ref[:relayed, :] = side_refs[0][...].astype(F32) + side_refs[1][...].astype(F32)
    sides_ref[relayed:, :] = side_refs[2][...].astype(F32) + side_refs[3][...].astype(F32)
    for place in range(comps // BLOCKC):
        rows, source = rows_of(place), rows_from(order_ref, place)
        for offset in range(0, share, XC):
            lanes = slice(offset, offset + XC)
            goal_ref[rows, lanes] = target_ref[rows, lanes] + sides_ref[source, lanes] * scale_ref[rows, :]
    sweep_steps(gs_ref, coef_ref, goal_ref, stacked_ref, value_ref, keep_ref)
    half = stacked_ref[:comps, :]
    sorted_ref[...] = half
    for place in range(comps // BLOCKC):
        half_ref[rows_from(order_ref, place), :] = stacked_ref[rows_of(place), :]
    store_products(half, movie_ref, joined_ref)


def store_products(half, movie_ref, joined_ref):
    frames = movie_ref.shape[1]
    joined_ref[:, :frames] = jnp.dot(half, movie_rows(movie_ref, half.shape[1]), preferred_element_type=F32)
    joined_ref[:, frames:] = lax.dot_general(half, half, BY_LAST, preferred_element_type=F32)


def product_kernel(half_ref, movie_ref, joined_ref):
    store_products(half_ref[...], movie_ref, joined_ref)


def chunk_kernel(stride, ours_ref, theirs_ref, *out_refs):
    rows = out_refs[0].shape[0]
    digit = lax.axis_index("vox") // stride % GROUP
    for index, out_ref in enumerate(out_refs):
        at = pl.ds(pl.multiple_of((digit ^ index) * rows, rows), rows)
        out_ref[...] = ours_ref[at, :] + theirs_ref[at, :]


def trace_kernel(order_ref, traces_ref, *refs):
    joined_refs, (out_ref, joined, goal_ref, gs_ref, coef_ref, stacked_ref, value_ref, sems) = refs[:-8], refs[-8:]
    comps, frames = traces_ref.shape
    digit = lax.axis_index("vox") % GROUP
    for index, ref in enumerate(joined_refs):
        rows = ref.shape[0]
        step = (GROUP - index) % GROUP
        place = pl.multiple_of((digit ^ step) * rows, rows) if rows < comps else 0
        joined[pl.ds(place, rows), :] = ref[...]
    cross = joined[:, frames:]
    eye, diagonal = diagonal_of(cross)
    inverse = 1.0 / (diagonal + ridge_weight)
    store_system(jnp.where(eye, 0.0, -cross * inverse), gs_ref, coef_ref)
    goal_ref[...] = joined[:, :frames] * inverse
    stacked_ref[:comps, :] = traces_ref[...]
    value_ref[...] = traces_ref[...].astype(F32)
    stacked_ref[comps:, :] = jnp.zeros((comps, frames), BF16)
    copies = [
        pltpu.make_async_copy(value_ref.at[rows_of(place), :], out_ref.at[rows_from(order_ref, place), :], sems.at[place])
        for place in range(comps // BLOCKC)
    ]
    sweep_steps(gs_ref, coef_ref, goal_ref, stacked_ref, value_ref, None, lambda place: copies[place].start())
    for copy in copies:
        copy.wait()


def in_hbm(array):
    return pltpu.with_memory_space_constraint(array, pltpu.HBM)


def swap(array):
    return lax.ppermute(array, "tm", [(0, 1), (1, 0)])


def from_group(arrays, stride):
    count = lax.axis_size("vox")
    return [lax.ppermute(array, "vox", [(i, i ^ (k * stride)) for i in range(count)]) for k, array in arrays]


def tree_sum(own, others):
    return (others[1] + others[2]) + (own + others[0])


def sum_over_vox(ours, theirs):
    comps, width = ours.shape
    rows = comps // GROUP
    top = lax.axis_size("vox") // GROUP
    chunks = pl.pallas_call(
        functools.partial(chunk_kernel, 1),
        out_shape=[shape_of((rows, width), F32)] * GROUP,
        in_specs=[VMEM] * 2,
        compiler_params=SMALL,
        out_specs=[VMEM] * GROUP,
    )(ours, theirs)
    mine = tree_sum(chunks[0], from_group([(k, chunks[k]) for k in range(1, GROUP)], 1))
    first, second, third = from_group([(k, mine) for k in range(1, GROUP)], top)
    mine = (mine + first) + (second + third)
    return [mine] + from_group([(k, mine) for k in range(1, GROUP)], 1)[::-1]


def local(movie, footprints, traces, support, block_order):
    comps, vox_local = footprints.shape
    frames = traces.shape[1]
    cores = lax.axis_size("tm")
    planes = lax.axis_size("vox")
    share = vox_local // cores
    me = lax.axis_index("tm")

    pairs = [(i, i ^ 1) for i in range(planes)]
    across = [(i, i + 1) for i in range(1, planes - 1, 2)] + [(i + 1, i) for i in range(1, planes - 1, 2)]
    onward = [(i, i + 2) for i in range(0, planes - 2, 2)] + [(i, i - 2) for i in range(3, planes, 2)]
    blocks = comps // BLOCKC
    relayed, direct, sorted_fp, support_rows, sorted_traces, movie_own = pl.pallas_call(
        load_kernel,
        out_shape=[
            shape_of((RELAYED, share), BF16),
            shape_of((comps - RELAYED, share), BF16),
            shape_of(footprints.shape, BF16),
            shape_of(support.shape[::-1], jnp.int32),
            shape_of(traces.shape, BF16),
            shape_of((share, frames), BF16),
        ],
        in_specs=[ANY] * 5,
        compiler_params=SMALL,
        out_specs=[VMEM] * 6,
        scratch_shapes=[pltpu.SMEM(block_order.shape, jnp.int32), pltpu.SemaphoreType.DMA((2 * blocks + 5,))],
    )(*[in_hbm(array) for array in (block_order, footprints, support.T, traces, movie)])
    beside_relayed = lax.ppermute(relayed, "vox", pairs)
    across_direct = lax.ppermute(direct, "vox", across)
    beside_direct = lax.ppermute(direct, "vox", pairs)
    sides = [beside_relayed, lax.ppermute(beside_relayed, "vox", onward), beside_direct, across_direct]

    smooth, keep, start = pl.pallas_call(
        smooth_kernel,
        out_shape=[shape_of((comps, share), F32)] * 3,
        in_specs=[SMEM] + [VMEM] * 2,
        compiler_params=SMALL,
        out_specs=[VMEM] * 3,
        scratch_shapes=[pltpu.VMEM((2 * comps, XC), F32)],
    )(in_hbm(block_order), sorted_fp, support_rows)

    if cores == 2:
        movies = [movie_own, swap(movie)]
        all_traces = [sorted_traces, swap(sorted_traces)]
    else:
        movies = [lax.all_to_all(movie, "tm", 0, 1, tiled=True)]
        all_traces = [lax.all_gather(sorted_traces, "tm", axis=1, tiled=True)]
    pieces = len(movies)
    table = (blocks, BLOCKC, BLOCKC, XC)
    target, system, coef, scale = pl.pallas_call(
        functools.partial(target_kernel, pieces),
        out_shape=[
            shape_of((comps, share), F32),
            shape_of((2 * comps, 2 * comps), BF16),
            shape_of(table, F32),
            shape_of((comps, XC), F32),
        ],
        in_specs=[VMEM] * (2 * pieces + 1),
        compiler_params=SMALL,
        out_specs=[VMEM] * 4,
    )(smooth, *all_traces, *movies)

    half, sorted_half, joined = pl.pallas_call(
        functools.partial(footprint_kernel, len(sides)),
        out_shape=[shape_of((comps, share), BF16)] * 2 + [shape_of((comps, movies[-1].shape[1] + comps), F32)],
        in_specs=[SMEM] + [VMEM] * (7 + len(sides)),
        compiler_params=SMALL,
        out_specs=[VMEM] * 3,
        scratch_shapes=[pltpu.VMEM((comps, share), F32)] * 2
        + [pltpu.VMEM((2 * comps, share), BF16), pltpu.VMEM((comps, share), F32)],
    )(block_order, target, keep, start, system, coef, scale, *sides, movies[-1])

    if cores == 2:
        theirs = swap(joined)
        ours = pl.pallas_call(
            product_kernel,
            out_shape=shape_of((comps, frames + comps), F32),
            in_specs=[VMEM] * 2,
            compiler_params=SMALL,
            out_specs=VMEM,
        )(sorted_half, movies[0])
        other = swap(half)
        new_footprints = jnp.where(
            me == 0, jnp.concatenate([half, other], axis=1), jnp.concatenate([other, half], axis=1)
        )
    else:
        projection = lax.psum_scatter(joined[:, : frames * cores], "tm", scatter_dimension=1, tiled=True)
        ours = jnp.concatenate([projection, lax.psum(joined[:, frames * cores :], "tm")], axis=1)
        theirs = jnp.zeros_like(ours)
        new_footprints = lax.all_gather(half, "tm", axis=1, tiled=True)

    if planes == GROUP * GROUP:
        joined = sum_over_vox(ours, theirs)
    else:
        joined = [lax.psum(ours + theirs, "vox")]
    new_traces = pl.pallas_call(
        trace_kernel,
        out_shape=shape_of((comps, frames), F32),
        in_specs=[SMEM] + [VMEM] * (len(joined) + 1),
        compiler_params=SMALL,
        out_specs=ANY,
        scratch_shapes=[
            pltpu.VMEM((comps, frames + comps), F32),
            pltpu.VMEM((comps, frames), F32),
            pltpu.VMEM((2 * comps, 2 * comps), BF16),
            pltpu.VMEM(table, F32),
            pltpu.VMEM((2 * comps, frames), BF16),
            pltpu.VMEM((comps, frames), F32),
            pltpu.SemaphoreType.DMA((blocks,)),
        ],
    )(block_order, sorted_traces, *joined)
    return (new_footprints, new_traces)


def solution(mesh):
    placed = (P("vox", "tm"), P(None, "vox"), P(None, "tm"), P(None, "vox"), P())
    return jax.shard_map(
        local,
        mesh=mesh,
        in_specs=placed,
        out_specs=(P(None, "vox"), P(None, "tm")),
        check_vma=False,
    )
```
